32 devices in a mesh: groups: 2 (over y), seq: 8 (over z, x), enc: 2 (over core).
Axes of the slice: x: 2, y: 2, z: 4, core: 2. Of those that a mesh axis runs over, the one named last changes fastest.
Arguments:
- self_queries: bfloat16 [2, 256, 4096], P('enc', ('groups', 'seq')), parts along dimension 1, may hold values from -32 to 32
- self_keys: bfloat16 [2, 256, 4096], P('enc', ('groups', 'seq')), parts along dimension 1, may hold values from -32 to 32
- self_values: bfloat16 [2, 256, 4096], P('enc', ('groups', 'seq')), parts along dimension 1, may hold values from -6 to 6
- text_queries: bfloat16 [2, 256, 4096], P('enc', ('groups', 'seq')), parts along dimension 1, may hold values from -32 to 32
- text_kv: bfloat16 [2, 2, 1024, 4096], P('enc', None, ('groups', 'seq')), parts along dimension 2, may hold values from -32 to 32
- text_len: int32 [4], P('groups'), parts along dimension 0, may hold values from 16 to 512
Outputs:
- self_mixed: bfloat16 [2, 256, 4096], P('enc', ('groups', 'seq')), parts along dimension 1
- text_mixed: bfloat16 [2, 256, 4096], P('enc', ('groups', 'seq')), parts along dimension 1
The draws below stay inside these ranges and needn't reach their ends.
There are 2 independent parts, one for each index of `groups`. The reference program is written for one: setup_inputs(seed, part) draws one part's arguments, and reference() takes and returns one part's arrays. A program takes and returns all parts, laid end to end along the dimension named above; each array names one. Nothing has to cross between parts.
Inputs may be any that keep to these rules, and one draw needn't show every extreme that they name: `text_len`: entry 0 is the prompt's length, entry 1 the negative prompt's; text rows at or past a length are padding.
All inputs are finite; a program needn't handle non-finite values.
Results may differ from the reference program's by a relative error of at most 0.0034.
Values may be sent and summed in bfloat16 or wider, within the bound.
A program may use at most 64 MiB of HBM per device.

```python
import math
import jax
import jax.numpy as jnp
from jax import lax

HEADS = 32
HEAD_DIM = 128
TEXT = 512
SEQ = 128
CHANNELS = 4096


def row_scaled(key, shape, scale):
    base = scale * jax.random.truncated_normal(jax.random.fold_in(key, 1), -4.0, 4.0, shape, jnp.float32)
    return base


def draw_self_queries(key, part):
    queries = row_scaled(jax.random.fold_in(key, 11), (2, SEQ, CHANNELS), 1.6)
    return queries.astype(jnp.bfloat16)


def draw_self_keys(key, part):
    key_table = row_scaled(jax.random.fold_in(key, 12), (2, SEQ, CHANNELS), 1.6)
    return key_table.astype(jnp.bfloat16)


def draw_text_queries(key, part):
    queries = row_scaled(jax.random.fold_in(key, 13), (2, SEQ, CHANNELS), 1.6)
    return queries.astype(jnp.bfloat16)


def draw_text_kv(key, part):
    key_table = row_scaled(jax.random.fold_in(key, 14), (2, TEXT, CHANNELS), 1.6)
    value_table = jax.random.truncated_normal(jax.random.fold_in(key, 15), -4.0, 4.0, (2, TEXT, CHANNELS), jnp.float32)
    return jnp.stack([key_table, value_table], axis=1).astype(jnp.bfloat16)


def block_levels(stream_key, dims, cuts, low, largest):
    loudness, own = 1.0, jax.random.fold_in(stream_key, 6)
    for position, blocks in cuts:
        steps = jnp.exp(jax.random.uniform(jax.random.fold_in(own, position), (blocks,), jnp.float32, low / len(cuts), largest / len(cuts)))
        loudness = loudness * jnp.repeat(steps, dims[position] // blocks).reshape([-1 if axis == position else 1 for axis in range(len(dims))])
    return loudness


def gaussian(stream_key, dims, scale, limit, shards=(), held_as=jnp.bfloat16):
    entries = scale * jax.random.normal(stream_key, dims, jnp.float32)
    if shards:
        entries = entries * block_levels(stream_key, dims, shards, -0.22, 0.18)
    return jnp.clip(entries, -limit, limit).astype(held_as)


def setup_inputs(seed: int = 0, part: int = 0) -> dict:
    key_list = jax.random.split(jax.random.key(seed), 7)
    own_keys = jax.random.split(jax.random.fold_in(key_list[6], part), 7)
    self_queries = draw_self_queries(jax.random.fold_in(jax.random.fold_in(key_list[6], part), 71), part)
    self_keys = draw_self_keys(jax.random.fold_in(jax.random.fold_in(key_list[6], part), 71), part)
    self_values = gaussian(own_keys[2], (2, SEQ, CHANNELS), 1.0, 6.0, ((0, 2), (1, 8)))
    text_queries = draw_text_queries(jax.random.fold_in(jax.random.fold_in(key_list[6], part), 71), part)
    text_kv = draw_text_kv(jax.random.fold_in(jax.random.fold_in(key_list[6], part), 71), part)
    text_len = jax.random.randint(own_keys[5], (2,), 16, TEXT + 1).astype(jnp.int32)
    return dict(self_queries=self_queries, self_keys=self_keys, self_values=self_values, text_queries=text_queries, text_kv=text_kv, text_len=text_len)


def head_attention(query_rows, key_rows, value_rows, live_mask):
    scores = jnp.dot(query_rows, key_rows.T, preferred_element_type=jnp.float32) / math.sqrt(HEAD_DIM)
    scores = jnp.where(live_mask[None, :], scores, -1e+30)
    shifted = jnp.where(live_mask[None, :], jnp.exp(scores - lax.optimization_barrier(jnp.max(scores, axis=1, keepdims=True))), 0.0)
    blended = jnp.dot(shifted.astype(jnp.bfloat16), value_rows, preferred_element_type=jnp.float32)
    return (blended / lax.optimization_barrier(jnp.sum(shifted, axis=1, keepdims=True))).astype(jnp.bfloat16)

def by_heads(tensor):
    return tensor.reshape(tensor.shape[0], HEADS, HEAD_DIM).transpose(1, 0, 2)

def from_heads(tensor):
    return tensor.transpose(1, 0, 2).reshape(tensor.shape[1], HEADS * HEAD_DIM)

def attend_all(queries, key_rows, value_rows, live_mask):

    def one_head(triple):
        return head_attention(triple[0], triple[1], triple[2], live_mask)
    return from_heads(lax.map(one_head, (by_heads(queries), by_heads(key_rows), by_heads(value_rows))))

def reference(self_queries, self_keys, self_values, text_queries, text_kv, text_len):
    self_list = []
    text_list = []
    positions = jnp.arange(TEXT, dtype=jnp.int32)
    every_key = jnp.ones((SEQ,), jnp.bool_)
    for branch in range(2):
        self_list.append(attend_all(self_queries[branch], self_keys[branch], self_values[branch], every_key))
        live_mask = positions < text_len[branch]
        text_list.append(attend_all(text_queries[branch], text_kv[branch, 0], text_kv[branch, 1], live_mask))
    return (jnp.stack(self_list), jnp.stack(text_list))
```

```python
import functools
import math

import jax
import jax.numpy as jnp
from jax import lax
from jax.experimental import pallas as pl
from jax.experimental.pallas import tpu as pltpu
from jax.sharding import PartitionSpec as P

HEADS = 32
HEAD_DIM = 128


def absorb(run_state, queries, key_rows, value_rows, live_mask):
    running_max, row_total, weighted_sum = run_state
    scores = jnp.einsum(
        "qpd,kpd->pqk", queries, key_rows, preferred_element_type=jnp.float32
    ) / math.sqrt(HEAD_DIM)
    scores = jnp.where(live_mask[None, None, :], scores, -1e30)
    new_max = jnp.maximum(running_max, jnp.max(scores, axis=2))
    weights = jnp.where(live_mask[None, None, :], jnp.exp(scores - new_max[:, :, None]), 0.0)
    factor = jnp.exp(running_max - new_max)
    row_total = row_total * factor + jnp.sum(weights, axis=2)
    weighted_sum = weighted_sum * factor[:, :, None] + jnp.einsum(
        "pqk,kpd->pqd", weights.astype(jnp.bfloat16), value_rows, preferred_element_type=jnp.float32
    )
    return (new_max, row_total, weighted_sum)


def empty_state(head_count, query_count):
    return (
        jnp.full((head_count, query_count), -1e30, jnp.float32),
        jnp.zeros((head_count, query_count), jnp.float32),
        jnp.zeros((head_count, query_count, HEAD_DIM), jnp.float32),
    )


def finish(run_state):
    running_max, row_total, weighted_sum = run_state
    return (weighted_sum / row_total[:, :, None]).transpose(1, 0, 2).astype(jnp.bfloat16)


def block_attention(queries, key_rows, value_rows, live_mask):
    query_total, heads_here, head_width = queries.shape
    key_total = key_rows.shape[0]
    key_block = 1024 if key_total % 1024 == 0 else key_total
    query_block = 512 if query_total % 512 == 0 else query_total
    key_blocks = key_rows.reshape(key_total // key_block, key_block, heads_here, head_width)
    value_blocks = value_rows.reshape(key_total // key_block, key_block, heads_here, head_width)
    live_blocks = live_mask.reshape(key_total // key_block, key_block)

    def one_block(query_piece):

        def absorb_block(run_state, pieces):
            return (absorb(run_state, query_piece, pieces[0], pieces[1], pieces[2]), None)

        final_state, unused = lax.scan(
            absorb_block,
            empty_state(heads_here, query_block),
            (key_blocks, value_blocks, live_blocks),
        )
        return finish(final_state)

    blended = lax.map(
        one_block, queries.reshape(query_total // query_block, query_block, heads_here, head_width)
    )
    return blended.reshape(query_total, heads_here, head_width)


def shards(self_queries, self_keys, self_values, text_queries, text_kv, text_len):
    token_rows = self_queries.shape[1]
    channel_count = self_queries.shape[2]
    seq_count = lax.axis_size("seq")
    quarter_count = max(seq_count // HEADS, 1)
    heads_here = max(HEADS // seq_count, 1)
    group_count = HEADS // heads_here
    head_span = heads_here * HEAD_DIM
    share_rows = token_rows // quarter_count
    query_total = share_rows * seq_count
    branch = lax.axis_index("enc")
    length = lax.dynamic_index_in_dim(text_len, branch, 0, keepdims=False)

    def head_view(tensor):
        return tensor.reshape(1, share_rows, seq_count, head_span)

    def repeated(tensor):
        spread = jnp.broadcast_to(
            tensor.reshape(1, token_rows, 1, group_count, head_span),
            (1, token_rows, quarter_count, group_count, head_span),
        )
        return spread.reshape(1, token_rows, seq_count, head_span)

    head_queries, head_keys, head_values = (
        lax.all_to_all(head_view(self_queries), "seq", split_axis=2, concat_axis=1, tiled=True),
        lax.all_to_all(repeated(self_keys), "seq", split_axis=2, concat_axis=1, tiled=True),
        lax.all_to_all(repeated(self_values), "seq", split_axis=2, concat_axis=1, tiled=True),
    )
    key_rows = head_keys.reshape(-1, heads_here, HEAD_DIM)
    value_rows = head_values.reshape(-1, heads_here, HEAD_DIM)
    query_rows = head_queries.reshape(query_total, heads_here, HEAD_DIM)
    every_key = jnp.ones((key_rows.shape[0],), jnp.bool_)
    self_heads = block_attention(query_rows, key_rows, value_rows, every_key)
    head_text_queries = lax.all_to_all(
        head_view(text_queries), "seq", split_axis=2, concat_axis=1, tiled=True
    )
    context_rows = text_kv.shape[2]
    spread = jnp.broadcast_to(
        text_kv.reshape(1, 2, context_rows, 1, group_count, head_span),
        (1, 2, context_rows, quarter_count, group_count, head_span),
    )
    head_context = lax.all_to_all(
        spread.reshape(1, 2, context_rows, seq_count, head_span),
        "seq",
        split_axis=3,
        concat_axis=2,
        tiled=True,
    )
    text_total = head_context.shape[2]
    context_keys = head_context[0, 0].reshape(text_total, heads_here, HEAD_DIM)
    context_values = head_context[0, 1].reshape(text_total, heads_here, HEAD_DIM)
    live_mask = jnp.arange(text_total, dtype=jnp.int32) < length
    text_heads = block_attention(
        head_text_queries.reshape(query_total, heads_here, HEAD_DIM),
        context_keys,
        context_values,
        live_mask,
    )
    self_view = self_heads.reshape(1, seq_count, share_rows, 1, head_span)
    text_view = text_heads.reshape(1, seq_count, share_rows, 1, head_span)
    self_back, text_back = (
        lax.all_to_all(self_view, "seq", split_axis=1, concat_axis=3, tiled=True),
        lax.all_to_all(text_view, "seq", split_axis=1, concat_axis=3, tiled=True),
    )
    self_mixed = self_back.reshape(1, token_rows, channel_count)
    text_mixed = text_back.reshape(1, token_rows, channel_count)
    return (self_mixed, text_mixed)


COLUMNS = 2
HALVES = 2
PLACES = 4
CHUNKS = 4
SENDS = (
    "query",
    "relay",
    "context",
    "self",
    "self_return",
    "near",
    "near_stat",
    "inbound",
    "inbound_stat",
    "joined",
    "joined_stat",
)
EARLY_OUTER, EARLY_INNER, LATER_INNER, LATE = (2, 4, 6), (6,), (2, 4), (7, 5, 3, 1)
ODD_AFTER = 0
JOINS = ((), (), (0,), (1,), (2, 3))
MESH = pl.DeviceIdType.MESH
FAR = -1e30


def attend(queries, key_rows, value_rows, live):
    scores = lax.dot_general(
        queries, key_rows, (((1,), (1,)), ((), ())), preferred_element_type=jnp.float32
    ) * (1.0 / math.sqrt(HEAD_DIM))
    if live is not None:
        scores = jnp.where(live, scores, FAR)
    top = jnp.max(scores, axis=1, keepdims=True)
    weights = jnp.exp(scores - top)
    if live is not None:
        weights = jnp.where(live, weights, 0.0)
    total = jnp.sum(weights, axis=1, keepdims=True)
    mixed = jnp.dot(weights.astype(jnp.bfloat16), value_rows, preferred_element_type=jnp.float32)
    return mixed, top, total


def fused(
    count,
    self_q,
    self_k,
    self_v,
    text_q,
    text_kv,
    text_len,
    self_out,
    text_back,
    stat_back,
    own,
    self_part,
    text_rows,
    context,
    text_part,
    inbound,
    joined,
    stat_part,
    stat_pack,
    stat_in,
    stat_join,
    stat_sum,
    query_recv,
    context_recv,
    inbound_recv,
    final_recv,
    sends,
    local_sem,
):
    me = lax.axis_index("seq")
    branch = lax.axis_index("enc")
    place, column = lax.div(me, COLUMNS), lax.rem(me, COLUMNS)
    half = lax.div(place, PLACES // HALVES)
    span = count // HALVES
    inner = lax.rem(place, 2) + half == 1
    outer = lax.rem(place, 2) + half != 1
    beside = COLUMNS * place + 1 - column
    near_place = place + 1 - 2 * lax.rem(place, 2)
    near, near_beside = COLUMNS * near_place + column, COLUMNS * near_place + 1 - column
    inner_there, outer_there = 2 - half, (PLACES - 1) * (1 - half)
    across = COLUMNS * inner_there + column
    there = (1 - half) * span
    rows = self_q.shape[1]
    query_total = count * rows
    context_rows = text_kv.shape[2]
    key_total = COLUMNS * context_rows
    self_span = own.shape[2]
    text_span = text_rows.shape[2]
    self_heads, text_heads = self_span // HEAD_DIM, text_span // HEAD_DIM
    chunk_heads = text_heads // CHUNKS
    chunk_span = chunk_heads * HEAD_DIM
    send_of = {name: sends.at[n] for n, name in enumerate(SENDS)}

    def self_cols(device):
        return pl.ds(pl.multiple_of(device * self_span, self_span), self_span)

    def text_cols(side):
        return pl.ds(pl.multiple_of(side * text_span, text_span), text_span)

    def part_cols(side, chunk, width=1):
        return pl.ds(pl.multiple_of(side * text_span + chunk * chunk_span, chunk_span), width * chunk_span)

    def piece(chunk, width=1):
        return pl.ds(chunk * chunk_span, width * chunk_span)

    def remote(source, target, kind, recv, device):
        return pltpu.make_async_remote_copy(
            src_ref=source,
            dst_ref=target,
            send_sem=send_of[kind],
            recv_sem=recv,
            device_id={"seq": device},
            device_id_type=MESH,
        )

    def take(ref, sem):
        pltpu.make_async_copy(ref, ref, sem).wait()

    def start(copies):
        for copy in copies:
            copy.start()

    def mirror(bits):
        far_place = (
            place,
            near_place,
            lax.rem(place + 2, PLACES),
            PLACES - 1 - place,
        )[bits // 2]
        return COLUMNS * far_place + (column if bits % 2 == 0 else 1 - column)

    kept_rows = pltpu.make_async_copy(text_q.at[0, :, text_cols(column)], text_rows.at[me], local_sem.at[0])
    kept_context = pltpu.make_async_copy(
        text_kv.at[0, :, :, text_cols(column)], context.at[column], local_sem.at[1]
    )
    kept_rows.start()
    kept_context.start()
    for kind, source in enumerate((self_q, self_k, self_v)):
        pltpu.make_async_copy(
            source.at[0, :, self_cols(me)], own.at[kind * count + me], local_sem.at[2]
        ).start()

    barrier = pltpu.get_barrier_semaphore()
    for step in range(1, count):
        pl.semaphore_signal(
            barrier, inc=1, device_id={"seq": lax.rem(me + step, count)}, device_id_type=MESH
        )
    with jax.named_scope("entry"):
        pl.semaphore_wait(barrier, count - 1)

    def held(origin, chunk):
        return text_rows.at[origin, :, piece(chunk)]

    def query_copy(kind, slot, chunk, source, origin, device):
        return remote(source, held(origin, chunk), kind, query_recv.at[slot, chunk], device)

    origins = [
        COLUMNS * inner_there + column,
        COLUMNS * outer_there + column,
        COLUMNS * inner_there + 1 - column,
        COLUMNS * outer_there + 1 - column,
    ]
    first = 2 + lax.rem(lax.rem(place, 2) + half + 1, 2)
    for chunk in range(CHUNKS):
        query_copy(
            "query", 0, chunk, text_q.at[0, :, part_cols(1 - column, chunk)], me, beside
        ).start()
    for chunk in range(CHUNKS):
        mine = text_q.at[0, :, part_cols(column, chunk)]
        query_copy("query", first, chunk, mine, me, across).start()
        query_copy("query", 1, chunk, mine, me, near).start()
    for chunk in range(CHUNKS):
        remote(
            text_kv.at[0, :, :, part_cols(1 - column, chunk)],
            context.at[column, :, :, piece(chunk)],
            "context",
            context_recv.at[chunk],
            beside,
        ).start()
    for chunk in range(CHUNKS):
        with jax.named_scope(f"q_beside{chunk}"):
            take(held(beside, chunk), query_recv.at[0, chunk])
        query_copy("query", first + 2, chunk, held(beside, chunk), beside, across).start()
        query_copy("query", 1, chunk, held(beside, chunk), beside, near).start()

    def start_self(bits):
        to = mirror(bits)
        for kind, source in enumerate((self_q, self_k, self_v)):
            remote(
                source.at[0, :, self_cols(to)], own.at[kind * count + me], "self", final_recv.at[3], to
            ).start()

    def far_waits(chunk):
        for n, origin in enumerate(origins):
            with jax.named_scope(f"q_far{chunk}{n}"):
                take(held(origin, chunk), query_recv.at[2 + n, chunk])
            yield n, origin

    @pl.when(outer)
    def _():
        for bits in EARLY_OUTER:
            start_self(bits)

    @pl.when(inner)
    def _():
        for bits in EARLY_INNER:
            start_self(bits)
        for chunk in range(CHUNKS):
            for n, origin in far_waits(chunk):
                query_copy("relay", 2 + n, chunk, held(origin, chunk), origin, near).start()
        for bits in LATER_INNER:
            start_self(bits)

    kept_rows.wait()

    length = text_len[branch]
    live = place * key_total + lax.broadcasted_iota(jnp.int32, (1, key_total), 1) < length
    lane = lax.broadcasted_iota(jnp.int32, (query_total, HEAD_DIM), 1)
    short_lane = lax.broadcasted_iota(jnp.int32, (rows, HEAD_DIM), 1)

    def gathered():
        packed = jnp.zeros((rows, HEAD_DIM), jnp.float32)
        for n in range(span):
            moved = stat_part[there + n]
            if n:
                moved = pltpu.roll(moved, n * text_heads, 1)
            packed = jnp.where(lax.div(short_lane, text_heads) == n, moved, packed)
        return packed

    def join(chunk):
        with jax.named_scope(f"inb{chunk}"):
            take(stat_in.at[chunk], inbound_recv.at[1, chunk])
            take(inbound.at[:, :, piece(chunk)], inbound_recv.at[0, chunk])
        sides = [gathered(), stat_in[chunk]]
        highest = jnp.maximum(*sides)
        shares = [jnp.exp(side - highest) for side in sides]
        whole = shares[0] + shares[1]
        shares = [share / whole for share in shares]
        ours = lax.div(lax.rem(short_lane, text_heads), chunk_heads) == chunk
        stat_sum[...] = jnp.where(ours, highest + jnp.log(whole), stat_sum[...])
        for n in range(span):
            for head in range(chunk * chunk_heads, (chunk + 1) * chunk_heads):
                cols = slice(head * HEAD_DIM, (head + 1) * HEAD_DIM)
                at = n * text_heads + head
                merged = (
                    text_part[there + n, :, cols].astype(jnp.float32) * shares[0][:, at : at + 1]
                    + inbound[n, :, cols].astype(jnp.float32) * shares[1][:, at : at + 1]
                )
                joined[n, :, cols] = merged.astype(jnp.bfloat16)
            remote(
                joined.at[n, :, piece(chunk)],
                text_back.at[HALVES, :, part_cols(column, chunk)],
                "joined",
                final_recv.at[0],
                there + n,
            ).start()
        if chunk == CHUNKS - 1:
            final = stat_sum[...]
            for n in range(span):
                stat_join[n] = pltpu.roll(final, HEAD_DIM - n * text_heads, 1) if n else final
                remote(
                    stat_join.at[n],
                    stat_back.at[HALVES, column],
                    "joined_stat",
                    final_recv.at[1],
                    there + n,
                ).start()

    neighbours = ((0, beside), (1, near), (1, near_beside))
    stats = jnp.full((query_total, HEAD_DIM), FAR, jnp.float32)

    @pl.when(inner)
    def _():
        stat_sum[...] = jnp.zeros_like(stat_sum)

    kept_context.wait()
    for chunk in range(CHUNKS):

        @pl.when(outer)
        def _(chunk=chunk):
            for _n in far_waits(chunk):
                pass

        with jax.named_scope(f"q_near{chunk}"):
            take(text_rows.at[pl.ds(0, 2), :, piece(chunk)], query_recv.at[1, chunk])
        with jax.named_scope(f"kv{chunk}"):
            take(context.at[0, :, :, piece(chunk)], context_recv.at[chunk])
        for head in range(chunk * chunk_heads, (chunk + 1) * chunk_heads):
            cols = slice(head * HEAD_DIM, (head + 1) * HEAD_DIM)
            mixed, top, total = attend(
                text_rows[:, :, cols].reshape(query_total, HEAD_DIM),
                context[:, 0, :, cols].reshape(key_total, HEAD_DIM),
                context[:, 1, :, cols].reshape(key_total, HEAD_DIM),
                live,
            )
            safe = jnp.where(total > 0.0, total, 1.0)
            weight = jnp.where(total > 0.0, top + jnp.log(safe), FAR)
            text_part[:, :, cols] = (mixed / safe).astype(jnp.bfloat16).reshape(count, rows, HEAD_DIM)
            stats = jnp.where(lane == head, weight, stats)
        stat_part[...] = stats.reshape(count, rows, HEAD_DIM)

        @pl.when(outer)
        def _(chunk=chunk):
            stat_pack[chunk] = gathered()
            remote(
                stat_pack.at[chunk], stat_in.at[chunk], "inbound_stat", inbound_recv.at[1, chunk], near
            ).start()
            remote(
                text_part.at[pl.ds(there, span), :, piece(chunk)],
                inbound.at[:, :, piece(chunk)],
                "inbound",
                inbound_recv.at[0, chunk],
                near,
            ).start()

        if chunk == ODD_AFTER:
            for bits in LATE:
                start_self(bits)
        if chunk % 2 == 1:
            for slot, device in neighbours:
                remote(
                    text_part.at[device, :, piece(chunk - 1, 2)],
                    text_back.at[slot, :, part_cols(column, chunk - 1, 2)],
                    "near",
                    final_recv.at[0],
                    device,
                ).start()
        for ready in JOINS[chunk]:

            @pl.when(inner)
            def _(ready=ready):
                join(ready)

    for slot, device in neighbours:
        remote(
            stat_part.at[device], stat_back.at[slot, column], "near_stat", final_recv.at[1], device
        ).start()
    kept_part = pltpu.make_async_copy(text_part.at[me], text_back.at[0, :, text_cols(column)], local_sem.at[0])
    kept_stat = pltpu.make_async_copy(stat_part.at[me], stat_back.at[0, column], local_sem.at[1])
    kept_part.start()
    kept_stat.start()

    take(own.at[pl.ds(0, 3)], local_sem.at[2])
    with jax.named_scope("self"):
        take(own.at[pl.ds(0, 3 * (count - 1))], final_recv.at[3])
    for head in range(self_heads):
        cols = slice(head * HEAD_DIM, (head + 1) * HEAD_DIM)
        mixed, top, total = attend(
            own[0:count, :, cols].reshape(query_total, HEAD_DIM),
            own[count : 2 * count, :, cols].reshape(query_total, HEAD_DIM),
            own[2 * count : 3 * count, :, cols].reshape(query_total, HEAD_DIM),
            None,
        )
        self_part[:, :, cols] = (mixed / total).astype(jnp.bfloat16).reshape(count, rows, HEAD_DIM)
    kept_self = pltpu.make_async_copy(self_part.at[me], self_out.at[0, :, self_cols(me)], local_sem.at[2])
    kept_self.start()
    for bits in (6, 7, 4, 5, 2, 3, 1):
        to = mirror(bits)
        remote(
            self_part.at[to], self_out.at[0, :, self_cols(me)], "self_return", final_recv.at[2], to
        ).start()
    for ready in JOINS[CHUNKS]:

        @pl.when(inner)
        def _(ready=ready):
            join(ready)

    kept_part.wait()
    kept_stat.wait()
    kept_self.wait()
    with jax.named_scope("back"):
        take(text_part.at[pl.ds(0, 3 + COLUMNS)], final_recv.at[0])
    with jax.named_scope("back_stat"):
        take(stat_part.at[pl.ds(0, 3 + COLUMNS)], final_recv.at[1])
    with jax.named_scope("self_out"):
        take(self_part.at[pl.ds(0, count - 1)], final_recv.at[2])
    with jax.named_scope("sends"):
        take(text_rows.at[pl.ds(0, 5)], send_of["query"])
        take(context.at[0], send_of["context"])
        take(own.at[pl.ds(0, 3 * (count - 1))], send_of["self"])
        take(self_part.at[pl.ds(0, count - 1)], send_of["self_return"])
        take(text_part.at[pl.ds(0, 3)], send_of["near"])
        take(stat_part.at[pl.ds(0, 3)], send_of["near_stat"])

    @pl.when(outer)
    def _():
        take(inbound, send_of["inbound"])
        take(stat_pack, send_of["inbound_stat"])

    @pl.when(inner)
    def _():
        take(text_rows.at[pl.ds(0, span)], send_of["relay"])
        take(joined, send_of["joined"])
        take(stat_join, send_of["joined_stat"])


def settle(self_in, text_in, stat_in, self_out, text_out, self_held, text_held, stat_held, mixed, in_sem, out_sem):
    channels = text_in.shape[2]
    text_span = channels // COLUMNS
    arrivals = [
        pltpu.make_async_copy(stat_in, stat_held, in_sem.at[0]),
        pltpu.make_async_copy(self_in, self_held, in_sem.at[1]),
    ]
    for side in range(COLUMNS):
        piece = pl.ds(side * text_span, text_span)
        arrivals.append(
            pltpu.make_async_copy(text_in.at[:, :, piece], text_held.at[:, :, piece], in_sem.at[2 + side])
        )
    for copy in arrivals:
        copy.start()
    leaving = [pltpu.make_async_copy(self_held, self_out, out_sem.at[0])]
    arrivals[0].wait()
    arrivals[1].wait()
    leaving[0].start()
    for side in range(COLUMNS):
        sides = [stat_held[n, side] for n in range(HALVES + 1)]
        highest = functools.reduce(jnp.maximum, sides)
        shares = [jnp.exp(each - highest) for each in sides]
        whole = sum(shares)
        shares = [share / whole for share in shares]
        arrivals[2 + side].wait()
        for head in range(text_span // HEAD_DIM):
            cols = slice(side * text_span + head * HEAD_DIM, side * text_span + (head + 1) * HEAD_DIM)
            merged = sum(
                text_held[n, :, cols].astype(jnp.float32) * shares[n][:, head : head + 1]
                for n in range(HALVES + 1)
            )
            mixed[0, :, cols] = merged.astype(jnp.bfloat16)
        piece = pl.ds(side * text_span, text_span)
        leaving.append(
            pltpu.make_async_copy(mixed.at[:, :, piece], text_out.at[:, :, piece], out_sem.at[1 + side])
        )
        leaving[1 + side].start()
    for copy in leaving:
        copy.wait()


def fused_shards(self_queries, self_keys, self_values, text_queries, text_kv, text_len):
    count = lax.axis_size("seq")
    rows, channels = self_queries.shape[1:]
    context_rows = text_kv.shape[2]
    span = count // HALVES
    self_span, text_span = channels // count, channels // COLUMNS
    in_place = pl.BlockSpec(memory_space=pl.ANY)
    bf16, f32 = jnp.bfloat16, jnp.float32
    out = jax.ShapeDtypeStruct((1, rows, channels), bf16)
    dma = pltpu.SemaphoreType.DMA
    results = pl.pallas_call(
        functools.partial(fused, count),
        out_shape=(
            out,
            jax.ShapeDtypeStruct((HALVES + 1, rows, channels), bf16),
            jax.ShapeDtypeStruct((HALVES + 1, COLUMNS, rows, HEAD_DIM), f32),
        ),
        in_specs=[in_place] * 5 + [pl.BlockSpec(memory_space=pltpu.SMEM)],
        out_specs=(in_place, in_place, in_place),
        scratch_shapes=[
            pltpu.VMEM((3 * count, rows, self_span), bf16),
            pltpu.VMEM((count, rows, self_span), bf16),
            pltpu.VMEM((count, rows, text_span), bf16),
            pltpu.VMEM((COLUMNS, 2, context_rows, text_span), bf16),
            pltpu.VMEM((count, rows, text_span), bf16),
            pltpu.VMEM((span, rows, text_span), bf16),
            pltpu.VMEM((span, rows, text_span), bf16),
            pltpu.VMEM((count, rows, HEAD_DIM), f32),
            pltpu.VMEM((CHUNKS, rows, HEAD_DIM), f32),
            pltpu.VMEM((CHUNKS, rows, HEAD_DIM), f32),
            pltpu.VMEM((span, rows, HEAD_DIM), f32),
            pltpu.VMEM((rows, HEAD_DIM), f32),
            dma((2 + span, CHUNKS)),
            dma((CHUNKS,)),
            dma((2, CHUNKS)),
            dma((4,)),
            dma((len(SENDS),)),
            dma((3,)),
        ],
        compiler_params=pltpu.CompilerParams(collective_id=0, has_side_effects=True),
        name="attention",
    )(self_queries, self_keys, self_values, text_queries, text_kv, text_len)
    return pl.pallas_call(
        settle,
        out_shape=(out, out),
        in_specs=[in_place] * 3,
        out_specs=(in_place, in_place),
        scratch_shapes=[
            pltpu.VMEM((1, rows, channels), bf16),
            pltpu.VMEM((HALVES + 1, rows, channels), bf16),
            pltpu.VMEM((HALVES + 1, COLUMNS, rows, HEAD_DIM), f32),
            pltpu.VMEM((1, rows, channels), bf16),
            dma((2 + COLUMNS,)),
            dma((1 + COLUMNS,)),
        ],
        name="settle",
    )(*results)


def solution(mesh):
    count = mesh.shape["seq"]
    fits = count == COLUMNS * PLACES and HEADS % count == 0
    return jax.shard_map(
        fused_shards if fits else shards,
        mesh=mesh,
        in_specs=(
            P("enc", ("groups", "seq"), None),
            P("enc", ("groups", "seq"), None),
            P("enc", ("groups", "seq"), None),
            P("enc", ("groups", "seq"), None),
            P("enc", None, ("groups", "seq"), None),
            P("groups"),
        ),
        out_specs=(P("enc", ("groups", "seq"), None), P("enc", ("groups", "seq"), None)),
        check_vma=False,
    )
```

```python
import functools
import math

import jax
import jax.numpy as jnp
from jax import lax
from jax.experimental import pallas as pl
from jax.experimental.pallas import tpu as pltpu
from jax.sharding import PartitionSpec as P

HEADS = 32
HEAD_DIM = 128


def absorb(run_state, queries, key_rows, value_rows, live_mask):
    running_max, row_total, weighted_sum = run_state
    scores = jnp.einsum(
        "qpd,kpd->pqk", queries, key_rows, preferred_element_type=jnp.float32
    ) / math.sqrt(HEAD_DIM)
    scores = jnp.where(live_mask[None, None, :], scores, -1e30)
    new_max = jnp.maximum(running_max, jnp.max(scores, axis=2))
    weights = jnp.where(live_mask[None, None, :], jnp.exp(scores - new_max[:, :, None]), 0.0)
    factor = jnp.exp(running_max - new_max)
    row_total = row_total * factor + jnp.sum(weights, axis=2)
    weighted_sum = weighted_sum * factor[:, :, None] + jnp.einsum(
        "pqk,kpd->pqd", weights.astype(jnp.bfloat16), value_rows, preferred_element_type=jnp.float32
    )
    return (new_max, row_total, weighted_sum)


def empty_state(head_count, query_count):
    return (
        jnp.full((head_count, query_count), -1e30, jnp.float32),
        jnp.zeros((head_count, query_count), jnp.float32),
        jnp.zeros((head_count, query_count, HEAD_DIM), jnp.float32),
    )


def finish(run_state):
    running_max, row_total, weighted_sum = run_state
    return (weighted_sum / row_total[:, :, None]).transpose(1, 0, 2).astype(jnp.bfloat16)


def block_attention(queries, key_rows, value_rows, live_mask):
    query_total, heads_here, head_width = queries.shape
    key_total = key_rows.shape[0]
    key_block = 1024 if key_total % 1024 == 0 else key_total
    query_block = 512 if query_total % 512 == 0 else query_total
    key_blocks = key_rows.reshape(key_total // key_block, key_block, heads_here, head_width)
    value_blocks = value_rows.reshape(key_total // key_block, key_block, heads_here, head_width)
    live_blocks = live_mask.reshape(key_total // key_block, key_block)

    def one_block(query_piece):

        def absorb_block(run_state, pieces):
            return (absorb(run_state, query_piece, pieces[0], pieces[1], pieces[2]), None)

        final_state, unused = lax.scan(
            absorb_block,
            empty_state(heads_here, query_block),
            (key_blocks, value_blocks, live_blocks),
        )
        return finish(final_state)

    blended = lax.map(
        one_block, queries.reshape(query_total // query_block, query_block, heads_here, head_width)
    )
    return blended.reshape(query_total, heads_here, head_width)


def shards(self_queries, self_keys, self_values, text_queries, text_kv, text_len):
    token_rows = self_queries.shape[1]
    channel_count = self_queries.shape[2]
    seq_count = lax.axis_size("seq")
    quarter_count = max(seq_count // HEADS, 1)
    heads_here = max(HEADS // seq_count, 1)
    group_count = HEADS // heads_here
    head_span = heads_here * HEAD_DIM
    share_rows = token_rows // quarter_count
    query_total = share_rows * seq_count
    branch = lax.axis_index("enc")
    length = lax.dynamic_index_in_dim(text_len, branch, 0, keepdims=False)

    def head_view(tensor):
        return tensor.reshape(1, share_rows, seq_count, head_span)

    def repeated(tensor):
        spread = jnp.broadcast_to(
            tensor.reshape(1, token_rows, 1, group_count, head_span),
            (1, token_rows, quarter_count, group_count, head_span),
        )
        return spread.reshape(1, token_rows, seq_count, head_span)

    head_queries, head_keys, head_values = (
        lax.all_to_all(head_view(self_queries), "seq", split_axis=2, concat_axis=1, tiled=True),
        lax.all_to_all(repeated(self_keys), "seq", split_axis=2, concat_axis=1, tiled=True),
        lax.all_to_all(repeated(self_values), "seq", split_axis=2, concat_axis=1, tiled=True),
    )
    key_rows = head_keys.reshape(-1, heads_here, HEAD_DIM)
    value_rows = head_values.reshape(-1, heads_here, HEAD_DIM)
    query_rows = head_queries.reshape(query_total, heads_here, HEAD_DIM)
    every_key = jnp.ones((key_rows.shape[0],), jnp.bool_)
    self_heads = block_attention(query_rows, key_rows, value_rows, every_key)
    head_text_queries = lax.all_to_all(
        head_view(text_queries), "seq", split_axis=2, concat_axis=1, tiled=True
    )
    context_rows = text_kv.shape[2]
    spread = jnp.broadcast_to(
        text_kv.reshape(1, 2, context_rows, 1, group_count, head_span),
        (1, 2, context_rows, quarter_count, group_count, head_span),
    )
    head_context = lax.all_to_all(
        spread.reshape(1, 2, context_rows, seq_count, head_span),
        "seq",
        split_axis=3,
        concat_axis=2,
        tiled=True,
    )
    text_total = head_context.shape[2]
    context_keys = head_context[0, 0].reshape(text_total, heads_here, HEAD_DIM)
    context_values = head_context[0, 1].reshape(text_total, heads_here, HEAD_DIM)
    live_mask = jnp.arange(text_total, dtype=jnp.int32) < length
    text_heads = block_attention(
        head_text_queries.reshape(query_total, heads_here, HEAD_DIM),
        context_keys,
        context_values,
        live_mask,
    )
    self_view = self_heads.reshape(1, seq_count, share_rows, 1, head_span)
    text_view = text_heads.reshape(1, seq_count, share_rows, 1, head_span)
    self_back, text_back = (
        lax.all_to_all(self_view, "seq", split_axis=1, concat_axis=3, tiled=True),
        lax.all_to_all(text_view, "seq", split_axis=1, concat_axis=3, tiled=True),
    )
    self_mixed = self_back.reshape(1, token_rows, channel_count)
    text_mixed = text_back.reshape(1, token_rows, channel_count)
    return (self_mixed, text_mixed)


COLUMNS = 2
HALVES = 2
PLACES = 4
CHUNKS = 4
GRANT = 12 * 1024 * 1024
SENDS = (
    "query",
    "relay",
    "context",
    "self",
    "self_return",
    "near",
    "near_stat",
    "inbound",
    "inbound_stat",
    "joined",
    "joined_stat",
)
OUTER = ('b2', 'b4', 'b6', 'c0', 'b7', 'b5', 'b3', 'b1', 'c1', 'c2', 'c3', 'n01', 'n23', 't', 's')
INNER = ('b6', 'r', 'b2', 'b4', 'c0', 'b7', 'b5', 'b3', 'b1', 'c1', 'n01', 'c2', 'j0', 'c3', 'n23', 'j1', 't', 's', 'j2', 'j3')
LATER = tuple(sorted(int(step[1]) for step in OUTER if step[0] == "x"))
MESH = pl.DeviceIdType.MESH
FAR = -1e30
SCALE = math.log2(math.e) / math.sqrt(HEAD_DIM)


def attend(queries, key_rows, value_rows, live):
    scores = lax.dot_general(
        queries, key_rows, (((1,), (1,)), ((), ())), preferred_element_type=jnp.float32
    )
    if live is not None:
        scores = jnp.where(live, scores, FAR)
    top = jnp.max(scores, axis=1, keepdims=True)
    weights = jnp.exp2((scores - top) * SCALE)
    total = jnp.sum(weights, axis=1, keepdims=True)
    mixed = jnp.dot(weights.astype(jnp.bfloat16), value_rows, preferred_element_type=jnp.float32)
    return mixed / total, top, total


def fused(
    count,
    self_q,
    self_k,
    self_v,
    text_q,
    text_kv,
    text_len,
    self_out,
    text_back,
    stat_back,
    own_back,
    own,
    self_part,
    text_rows,
    context,
    text_part,
    text_full,
    inbound,
    joined,
    stat_part,
    stat_pack,
    stat_in,
    stat_join,
    stat_sum,
    live_len,
    query_recv,
    context_recv,
    inbound_recv,
    final_recv,
    sends,
    local_sem,
):
    me = lax.axis_index("seq")
    branch = lax.axis_index("enc")
    place, column = lax.div(me, COLUMNS), lax.rem(me, COLUMNS)
    half = lax.div(place, PLACES // HALVES)
    span = count // HALVES
    inner = lax.rem(place, 2) + half == 1
    outer = lax.rem(place, 2) + half != 1
    beside = COLUMNS * place + 1 - column
    near_place = place + 1 - 2 * lax.rem(place, 2)
    near, near_beside = COLUMNS * near_place + column, COLUMNS * near_place + 1 - column
    inner_there, outer_there = 2 - half, (PLACES - 1) * (1 - half)
    across = COLUMNS * inner_there + column
    there = (1 - half) * span
    rows = self_q.shape[1]
    query_total = count * rows
    context_rows = text_kv.shape[2]
    key_total = COLUMNS * context_rows
    self_span = own.shape[2]
    text_span = text_rows.shape[2]
    self_heads, text_heads = self_span // HEAD_DIM, text_span // HEAD_DIM
    chunk_heads = text_heads // CHUNKS
    chunk_span = chunk_heads * HEAD_DIM
    send_of = {name: sends.at[n] for n, name in enumerate(SENDS)}

    def self_cols(device):
        return pl.ds(pl.multiple_of(device * self_span, self_span), self_span)

    def text_cols(side):
        return pl.ds(pl.multiple_of(side * text_span, text_span), text_span)

    def part_cols(side, chunk, width=1):
        return pl.ds(pl.multiple_of(side * text_span + chunk * chunk_span, chunk_span), width * chunk_span)

    def piece(chunk, width=1):
        return pl.ds(chunk * chunk_span, width * chunk_span)

    def remote(source, target, kind, recv, device):
        return pltpu.make_async_remote_copy(
            src_ref=source,
            dst_ref=target,
            send_sem=send_of[kind],
            recv_sem=recv,
            device_id={"seq": device},
            device_id_type=MESH,
        )

    def take(ref, sem):
        pltpu.make_async_copy(ref, ref, sem).wait()

    def start(copies):
        for copy in copies:
            copy.start()

    def mirror(bits):
        far_place = (
            place,
            near_place,
            lax.rem(place + 2, PLACES),
            PLACES - 1 - place,
        )[bits // 2]
        return COLUMNS * far_place + (column if bits % 2 == 0 else 1 - column)

    barrier = pltpu.get_barrier_semaphore()
    for step in range(1, count):
        pl.semaphore_signal(
            barrier, inc=1, device_id={"seq": lax.rem(me + step, count)}, device_id_type=MESH
        )
    kept_len = pltpu.make_async_copy(text_len, live_len, local_sem.at[3])
    kept_rows = pltpu.make_async_copy(text_q.at[0, :, text_cols(column)], text_rows.at[me], local_sem.at[0])
    kept_context = pltpu.make_async_copy(
        text_kv.at[0, :, :, text_cols(column)], context.at[column], local_sem.at[1]
    )
    kept_len.start()
    kept_rows.start()
    kept_context.start()
    for kind, source in enumerate((self_q, self_k, self_v)):
        pltpu.make_async_copy(
            source.at[0, :, self_cols(me)], own.at[kind * count + me], local_sem.at[2]
        ).start()

    with jax.named_scope("entry"):
        pl.semaphore_wait(barrier, count - 1)

    def held(origin, chunk):
        return text_rows.at[origin, :, piece(chunk)]

    def query_copy(kind, slot, chunk, source, origin, device):
        return remote(source, held(origin, chunk), kind, query_recv.at[slot, chunk], device)

    origins = [
        COLUMNS * inner_there + column,
        COLUMNS * outer_there + column,
        COLUMNS * inner_there + 1 - column,
        COLUMNS * outer_there + 1 - column,
    ]
    first = 2 + lax.rem(lax.rem(place, 2) + half + 1, 2)
    for chunk in range(CHUNKS):
        query_copy(
            "query", 0, chunk, text_q.at[0, :, part_cols(1 - column, chunk)], me, beside
        ).start()
    for chunk in range(CHUNKS):
        mine = text_q.at[0, :, part_cols(column, chunk)]
        query_copy("query", first, chunk, mine, me, across).start()
        query_copy("query", 1, chunk, mine, me, near).start()
    def context_send(chunk):
        remote(
            text_kv.at[0, :, :, part_cols(1 - column, chunk)],
            context.at[column, :, :, piece(chunk)],
            "context",
            context_recv.at[chunk],
            beside,
        ).start()

    for chunk in range(CHUNKS):
        if chunk not in LATER:
            context_send(chunk)

    @pl.when(branch == 0)
    def _():
        for chunk in LATER:
            context_send(chunk)

    for chunk in range(CHUNKS):
        with jax.named_scope(f"q_beside{chunk}"):
            take(held(beside, chunk), query_recv.at[0, chunk])
        query_copy("query", first + 2, chunk, held(beside, chunk), beside, across).start()
        query_copy("query", 1, chunk, held(beside, chunk), beside, near).start()

    def start_self(bits):
        to = mirror(bits)
        for kind, source in enumerate((self_q, self_k, self_v)):
            remote(
                source.at[0, :, self_cols(to)], own.at[kind * count + me], "self", final_recv.at[3], to
            ).start()

    def far_waits(chunk):
        for n, origin in enumerate(origins):
            with jax.named_scope(f"q_far{chunk}{n}"):
                take(held(origin, chunk), query_recv.at[2 + n, chunk])
            yield n, origin

    kept_rows.wait()

    kept_len.wait()
    length = live_len[branch]
    live = place * key_total + lax.broadcasted_iota(jnp.int32, (1, key_total), 1) < length
    lane = lax.broadcasted_iota(jnp.int32, (query_total, HEAD_DIM), 1)
    short_lane = lax.broadcasted_iota(jnp.int32, (rows, HEAD_DIM), 1)

    def gathered():
        packed = jnp.zeros((rows, HEAD_DIM), jnp.float32)
        for n in range(span):
            moved = stat_part[there + n]
            if n:
                moved = pltpu.roll(moved, n * text_heads, 1)
            packed = jnp.where(lax.div(short_lane, text_heads) == n, moved, packed)
        return packed

    def join(chunk):
        with jax.named_scope(f"inb{chunk}"):
            take(stat_in.at[chunk], inbound_recv.at[1, chunk])
            take(inbound.at[:, :, piece(chunk)], inbound_recv.at[0, chunk])
        sides = [gathered(), stat_in[chunk]]
        highest = jnp.maximum(*sides)
        shares = [jnp.exp2(side - highest) for side in sides]
        whole = shares[0] + shares[1]
        shares = [share / whole for share in shares]
        ours = lax.div(lax.rem(short_lane, text_heads), chunk_heads) == chunk
        final = jnp.where(ours, highest + jnp.log2(whole), stat_sum[...])
        stat_sum[...] = final
        for n in range(span):
            if chunk == CHUNKS - 1:
                stat_join[n] = pltpu.roll(final, HEAD_DIM - n * text_heads, 1) if n else final
                remote(
                    stat_join.at[n],
                    stat_back.at[HALVES, column],
                    "joined_stat",
                    final_recv.at[1],
                    there + n,
                ).start()
        for n in range(span):
            for head in range(chunk * chunk_heads, (chunk + 1) * chunk_heads):
                cols = slice(head * HEAD_DIM, (head + 1) * HEAD_DIM)
                at = n * text_heads + head
                merged = (
                    text_full[there + n, :, cols] * shares[0][:, at : at + 1]
                    + inbound[n, :, cols].astype(jnp.float32) * shares[1][:, at : at + 1]
                )
                joined[n, :, cols] = merged.astype(jnp.bfloat16)
            remote(
                joined.at[n, :, piece(chunk)],
                text_back.at[HALVES, :, part_cols(column, chunk)],
                "joined",
                final_recv.at[0],
                there + n,
            ).start()

    neighbours = ((0, beside), (1, near), (1, near_beside))

    def text_chunk(chunk, role):
        if role == "outer":
            for _n in far_waits(chunk):
                pass
        with jax.named_scope(f"q_near{chunk}"):
            take(text_rows.at[pl.ds(0, 2), :, piece(chunk)], query_recv.at[1, chunk])
        with jax.named_scope(f"kv{chunk}"):
            take(context.at[0, :, :, piece(chunk)], context_recv.at[chunk])
        tops, totals = jnp.full((query_total, HEAD_DIM), FAR, jnp.float32), 1.0
        for head in range(chunk * chunk_heads, (chunk + 1) * chunk_heads):
            cols = slice(head * HEAD_DIM, (head + 1) * HEAD_DIM)
            mixed, top, total = attend(
                text_rows[:, :, cols].reshape(query_total, HEAD_DIM),
                context[:, 0, :, cols].reshape(key_total, HEAD_DIM),
                context[:, 1, :, cols].reshape(key_total, HEAD_DIM),
                live,
            )
            share = mixed.reshape(count, rows, HEAD_DIM)
            text_full[:, :, cols] = share
            text_part[:, :, cols] = share.astype(jnp.bfloat16)
            tops = jnp.where(lane == head, top, tops)
            totals = jnp.where(lane == head, total, totals)
        if role == "outer":
            remote(
                text_part.at[pl.ds(there, span), :, piece(chunk)],
                inbound.at[:, :, piece(chunk)],
                "inbound",
                inbound_recv.at[0, chunk],
                near,
            ).start()
        levels = (tops * SCALE + jnp.log2(totals)).reshape(count, rows, HEAD_DIM)
        if chunk:
            before = lax.broadcasted_iota(jnp.int32, (1, 1, HEAD_DIM), 2) < chunk * chunk_heads
            levels = jnp.where(before, stat_part[...], levels)
        stat_part[...] = levels
        if role == "outer":
            stat_pack[chunk] = gathered()
            remote(
                stat_pack.at[chunk], stat_in.at[chunk], "inbound_stat", inbound_recv.at[1, chunk], near
            ).start()

    def near_send(low, high):
        for slot, device in neighbours:
            remote(
                text_part.at[device, :, piece(low, high + 1 - low)],
                text_back.at[slot, :, part_cols(column, low, high + 1 - low)],
                "near",
                final_recv.at[0],
                device,
            ).start()

    def near_stats():
        for slot, device in neighbours:
            remote(
                stat_part.at[device], stat_back.at[slot, column], "near_stat", final_recv.at[1], device
            ).start()

    def self_attention():
        take(own.at[pl.ds(0, 3)], local_sem.at[2])
        with jax.named_scope("self"):
            take(own.at[pl.ds(0, 3 * (count - 1))], final_recv.at[3])
        for head in range(self_heads):
            cols = slice(head * HEAD_DIM, (head + 1) * HEAD_DIM)
            mixed, _, _ = attend(
                own[0:count, :, cols].reshape(query_total, HEAD_DIM),
                own[count : 2 * count, :, cols].reshape(query_total, HEAD_DIM),
                own[2 * count : 3 * count, :, cols].reshape(query_total, HEAD_DIM),
                None,
            )
            self_part[:, :, cols] = mixed.astype(jnp.bfloat16).reshape(count, rows, HEAD_DIM)
        for n in range(count - 1):
            to = n + lax.div(n + count - me, count)
            remote(
                self_part.at[to], self_out.at[0, :, self_cols(me)], "self_return", final_recv.at[2], to
            ).start()

    def relay():
        for chunk in range(CHUNKS):
            for n, origin in far_waits(chunk):
                query_copy("relay", 2 + n, chunk, held(origin, chunk), origin, near).start()

    def run(role, steps):
        for step in steps:
            name, _, only = step.partition(".")
            kind, digits = name[0], [int(digit) for digit in name[1:]]
            action = {
                "b": start_self,
                "x": context_send,
                "c": functools.partial(text_chunk, role=role),
                "n": near_send,
                "j": join,
                "r": relay,
                "t": near_stats,
                "s": self_attention,
            }[kind]
            if only:
                pl.when(branch == int(only))(functools.partial(action, *digits))
            else:
                action(*digits)

    kept_context.wait()

    @pl.when(outer)
    def _():
        run("outer", OUTER)

    @pl.when(inner)
    def _():
        stat_sum[...] = jnp.zeros_like(stat_sum)
        run("inner", INNER)

    kept_part = pltpu.make_async_copy(text_full.at[me], own_back, local_sem.at[0])
    kept_stat = pltpu.make_async_copy(stat_part.at[me], stat_back.at[0, column], local_sem.at[1])
    kept_self = pltpu.make_async_copy(self_part.at[me], self_out.at[0, :, self_cols(me)], local_sem.at[2])
    kept_part.start()
    kept_stat.start()
    kept_self.start()
    kept_part.wait()
    kept_stat.wait()
    kept_self.wait()
    with jax.named_scope("back"):
        take(text_part.at[pl.ds(0, 3 + COLUMNS)], final_recv.at[0])
    with jax.named_scope("back_stat"):
        take(stat_part.at[pl.ds(0, 3 + COLUMNS)], final_recv.at[1])
    with jax.named_scope("self_out"):
        take(self_part.at[pl.ds(0, count - 1)], final_recv.at[2])
    with jax.named_scope("sends"):
        take(text_rows.at[pl.ds(0, 5)], send_of["query"])
        take(context.at[0], send_of["context"])
        take(own.at[pl.ds(0, 3 * (count - 1))], send_of["self"])
        take(self_part.at[pl.ds(0, count - 1)], send_of["self_return"])
        take(text_part.at[pl.ds(0, 3)], send_of["near"])
        take(stat_part.at[pl.ds(0, 3)], send_of["near_stat"])

    @pl.when(outer)
    def _():
        take(inbound, send_of["inbound"])
        take(stat_pack, send_of["inbound_stat"])

    @pl.when(inner)
    def _():
        take(text_rows.at[pl.ds(0, span)], send_of["relay"])
        take(joined, send_of["joined"])
        take(stat_join, send_of["joined_stat"])


def settle(self_in, text_in, stat_in, own_in, self_out, text_out, mixed, out_sem):
    column = lax.rem(lax.axis_index("seq"), COLUMNS)
    text_span = own_in.shape[1]
    leaving = [pltpu.make_async_copy(self_in, self_out, out_sem.at[0])]
    leaving[0].start()
    for side in range(COLUMNS):
        sides = [stat_in[n, side] for n in range(HALVES + 1)]
        highest = functools.reduce(jnp.maximum, sides)
        shares = [jnp.exp2(each - highest) for each in sides]
        whole = sum(shares)
        shares = [share / whole for share in shares]
        for head in range(text_span // HEAD_DIM):
            cols = slice(side * text_span + head * HEAD_DIM, side * text_span + (head + 1) * HEAD_DIM)
            here = jnp.where(
                column == side,
                own_in[:, head * HEAD_DIM : (head + 1) * HEAD_DIM],
                text_in[0, :, cols].astype(jnp.float32),
            )
            merged = here * shares[0][:, head : head + 1] + sum(
                text_in[n, :, cols].astype(jnp.float32) * shares[n][:, head : head + 1]
                for n in range(1, HALVES + 1)
            )
            mixed[0, :, cols] = merged.astype(jnp.bfloat16)
        piece = pl.ds(side * text_span, text_span)
        leaving.append(
            pltpu.make_async_copy(mixed.at[:, :, piece], text_out.at[:, :, piece], out_sem.at[1 + side])
        )
        leaving[1 + side].start()
    for copy in leaving:
        copy.wait()


def fused_shards(self_queries, self_keys, self_values, text_queries, text_kv, text_len):
    count = lax.axis_size("seq")
    rows, channels = self_queries.shape[1:]
    context_rows = text_kv.shape[2]
    span = count // HALVES
    self_span, text_span = channels // count, channels // COLUMNS
    operands = (self_queries, self_keys, self_values, text_queries, text_kv, text_len)
    in_place = pl.BlockSpec(memory_space=pl.ANY)
    bf16, f32 = jnp.bfloat16, jnp.float32
    out = jax.ShapeDtypeStruct((1, rows, channels), bf16)
    dma = pltpu.SemaphoreType.DMA
    results = pl.pallas_call(
        functools.partial(fused, count),
        out_shape=(
            out,
            jax.ShapeDtypeStruct((HALVES + 1, rows, channels), bf16),
            jax.ShapeDtypeStruct((HALVES + 1, COLUMNS, rows, HEAD_DIM), f32),
            jax.ShapeDtypeStruct((rows, text_span), f32),
        ),
        in_specs=[in_place] * 6,
        out_specs=(in_place,) * 4,
        scratch_shapes=[
            pltpu.VMEM((3 * count, rows, self_span), bf16),
            pltpu.VMEM((count, rows, self_span), bf16),
            pltpu.VMEM((count, rows, text_span), bf16),
            pltpu.VMEM((COLUMNS, 2, context_rows, text_span), bf16),
            pltpu.VMEM((count, rows, text_span), bf16),
            pltpu.VMEM((count, rows, text_span), f32),
            pltpu.VMEM((span, rows, text_span), bf16),
            pltpu.VMEM((span, rows, text_span), bf16),
            pltpu.VMEM((count, rows, HEAD_DIM), f32),
            pltpu.VMEM((CHUNKS, rows, HEAD_DIM), f32),
            pltpu.VMEM((CHUNKS, rows, HEAD_DIM), f32),
            pltpu.VMEM((span, rows, HEAD_DIM), f32),
            pltpu.VMEM((rows, HEAD_DIM), f32),
            pltpu.SMEM(text_len.shape, jnp.int32),
            dma((2 + span, CHUNKS)),
            dma((CHUNKS,)),
            dma((2, CHUNKS)),
            dma((4,)),
            dma((len(SENDS),)),
            dma((4,)),
        ],
        compiler_params=pltpu.CompilerParams(
            collective_id=0, has_side_effects=True, vmem_limit_bytes=GRANT
        ),
        name="attention",
    )(*[pltpu.with_memory_space_constraint(each, pltpu.HBM) for each in operands])
    return pl.pallas_call(
        settle,
        out_shape=(out, out),
        in_specs=[pl.BlockSpec(memory_space=pltpu.VMEM)] * 4,
        out_specs=(in_place, in_place),
        scratch_shapes=[pltpu.VMEM((1, rows, channels), bf16), dma((1 + COLUMNS,))],
        compiler_params=pltpu.CompilerParams(vmem_limit_bytes=GRANT),
        name="settle",
    )(*results)


def solution(mesh):
    count = mesh.shape["seq"]
    fits = count == COLUMNS * PLACES and HEADS % count == 0
    return jax.shard_map(
        fused_shards if fits else shards,
        mesh=mesh,
        in_specs=(
            P("enc", ("groups", "seq"), None),
            P("enc", ("groups", "seq"), None),
            P("enc", ("groups", "seq"), None),
            P("enc", ("groups", "seq"), None),
            P("enc", None, ("groups", "seq"), None),
            P("groups"),
        ),
        out_specs=(P("enc", ("groups", "seq"), None), P("enc", ("groups", "seq"), None)),
        check_vma=False,
    )
```

```python
import functools
import math

import jax
import jax.numpy as jnp
from jax import lax
from jax.experimental import pallas as pl
from jax.experimental.pallas import tpu as pltpu
from jax.sharding import PartitionSpec as P

HEADS = 32
HEAD_DIM = 128


def absorb(run_state, queries, key_rows, value_rows, live_mask):
    running_max, row_total, weighted_sum = run_state
    scores = jnp.einsum(
        "qpd,kpd->pqk", queries, key_rows, preferred_element_type=jnp.float32
    ) / math.sqrt(HEAD_DIM)
    scores = jnp.where(live_mask[None, None, :], scores, -1e30)
    new_max = jnp.maximum(running_max, jnp.max(scores, axis=2))
    weights = jnp.where(live_mask[None, None, :], jnp.exp(scores - new_max[:, :, None]), 0.0)
    factor = jnp.exp(running_max - new_max)
    row_total = row_total * factor + jnp.sum(weights, axis=2)
    weighted_sum = weighted_sum * factor[:, :, None] + jnp.einsum(
        "pqk,kpd->pqd", weights.astype(jnp.bfloat16), value_rows, preferred_element_type=jnp.float32
    )
    return (new_max, row_total, weighted_sum)


def empty_state(head_count, query_count):
    return (
        jnp.full((head_count, query_count), -1e30, jnp.float32),
        jnp.zeros((head_count, query_count), jnp.float32),
        jnp.zeros((head_count, query_count, HEAD_DIM), jnp.float32),
    )


def finish(run_state):
    running_max, row_total, weighted_sum = run_state
    return (weighted_sum / row_total[:, :, None]).transpose(1, 0, 2).astype(jnp.bfloat16)


def block_attention(queries, key_rows, value_rows, live_mask):
    query_total, heads_here, head_width = queries.shape
    key_total = key_rows.shape[0]
    key_block = 1024 if key_total % 1024 == 0 else key_total
    query_block = 512 if query_total % 512 == 0 else query_total
    key_blocks = key_rows.reshape(key_total // key_block, key_block, heads_here, head_width)
    value_blocks = value_rows.reshape(key_total // key_block, key_block, heads_here, head_width)
    live_blocks = live_mask.reshape(key_total // key_block, key_block)

    def one_block(query_piece):

        def absorb_block(run_state, pieces):
            return (absorb(run_state, query_piece, pieces[0], pieces[1], pieces[2]), None)

        final_state, unused = lax.scan(
            absorb_block,
            empty_state(heads_here, query_block),
            (key_blocks, value_blocks, live_blocks),
        )
        return finish(final_state)

    blended = lax.map(
        one_block, queries.reshape(query_total // query_block, query_block, heads_here, head_width)
    )
    return blended.reshape(query_total, heads_here, head_width)


def shards(self_queries, self_keys, self_values, text_queries, text_kv, text_len):
    token_rows = self_queries.shape[1]
    channel_count = self_queries.shape[2]
    seq_count = lax.axis_size("seq")
    quarter_count = max(seq_count // HEADS, 1)
    heads_here = max(HEADS // seq_count, 1)
    group_count = HEADS // heads_here
    head_span = heads_here * HEAD_DIM
    share_rows = token_rows // quarter_count
    query_total = share_rows * seq_count
    branch = lax.axis_index("enc")
    length = lax.dynamic_index_in_dim(text_len, branch, 0, keepdims=False)

    def head_view(tensor):
        return tensor.reshape(1, share_rows, seq_count, head_span)

    def repeated(tensor):
        spread = jnp.broadcast_to(
            tensor.reshape(1, token_rows, 1, group_count, head_span),
            (1, token_rows, quarter_count, group_count, head_span),
        )
        return spread.reshape(1, token_rows, seq_count, head_span)

    head_queries, head_keys, head_values = (
        lax.all_to_all(head_view(self_queries), "seq", split_axis=2, concat_axis=1, tiled=True),
        lax.all_to_all(repeated(self_keys), "seq", split_axis=2, concat_axis=1, tiled=True),
        lax.all_to_all(repeated(self_values), "seq", split_axis=2, concat_axis=1, tiled=True),
    )
    key_rows = head_keys.reshape(-1, heads_here, HEAD_DIM)
    value_rows = head_values.reshape(-1, heads_here, HEAD_DIM)
    query_rows = head_queries.reshape(query_total, heads_here, HEAD_DIM)
    every_key = jnp.ones((key_rows.shape[0],), jnp.bool_)
    self_heads = block_attention(query_rows, key_rows, value_rows, every_key)
    head_text_queries = lax.all_to_all(
        head_view(text_queries), "seq", split_axis=2, concat_axis=1, tiled=True
    )
    context_rows = text_kv.shape[2]
    spread = jnp.broadcast_to(
        text_kv.reshape(1, 2, context_rows, 1, group_count, head_span),
        (1, 2, context_rows, quarter_count, group_count, head_span),
    )
    head_context = lax.all_to_all(
        spread.reshape(1, 2, context_rows, seq_count, head_span),
        "seq",
        split_axis=3,
        concat_axis=2,
        tiled=True,
    )
    text_total = head_context.shape[2]
    context_keys = head_context[0, 0].reshape(text_total, heads_here, HEAD_DIM)
    context_values = head_context[0, 1].reshape(text_total, heads_here, HEAD_DIM)
    live_mask = jnp.arange(text_total, dtype=jnp.int32) < length
    text_heads = block_attention(
        head_text_queries.reshape(query_total, heads_here, HEAD_DIM),
        context_keys,
        context_values,
        live_mask,
    )
    self_view = self_heads.reshape(1, seq_count, share_rows, 1, head_span)
    text_view = text_heads.reshape(1, seq_count, share_rows, 1, head_span)
    self_back, text_back = (
        lax.all_to_all(self_view, "seq", split_axis=1, concat_axis=3, tiled=True),
        lax.all_to_all(text_view, "seq", split_axis=1, concat_axis=3, tiled=True),
    )
    self_mixed = self_back.reshape(1, token_rows, channel_count)
    text_mixed = text_back.reshape(1, token_rows, channel_count)
    return (self_mixed, text_mixed)


COLUMNS = 2
HALVES = 2
PLACES = 4
CHUNKS = 4
GRANT = 12 * 1024 * 1024
SENDS = {"query": 0, "context": 0, "near": 0, "self": 1, "self_return": 1}
SENDS |= {"relay": 2, "joined": 2, "inbound": 2, "near_stat": 3, "inbound_stat": 3, "joined_stat": 3}
OUTER = ('b2', 'b4', 'b6.1', 'c0', 'b6.0', 'b7', 'b5', 'b3', 'b1', 'c1', 'c2', 'c3', 'n01', 'n23', 't', 's')
INNER = ('b6', 'r', 'b2', 'b4.1', 'c0', 'b4.0', 'b7', 'b5', 'b3', 'b1', 'c1', 'c2', 'j0', 'c3', 'n01', 'n23', 'j1', 't', 's', 'j2', 'j3')
FIRST_OUTER, FIRST_INNER = (), ()
LATER = tuple(sorted(int(step[1]) for step in OUTER if step[0] == "x"))
MESH = pl.DeviceIdType.MESH
FAR = -1e30
SCALE = math.log2(math.e) / math.sqrt(HEAD_DIM)


def attend(loads, heads, live):
    scores, sides = {}, {}
    for head in heads:
        queries, key_rows, _ = loads(head)
        scores[head] = lax.dot_general(
            queries, key_rows, (((1,), (1,)), ((), ())), preferred_element_type=jnp.float32
        )
    for head in heads:
        held = scores[head] if live is None else jnp.where(live, scores[head], FAR)
        top = jnp.max(held, axis=1, keepdims=True)
        weights = jnp.exp2((held - top) * SCALE)
        sides[head] = weights.astype(jnp.bfloat16), top, jnp.sum(weights, axis=1, keepdims=True)
    for head in heads:
        weights, top, total = sides[head]
        mixed = jnp.dot(weights, loads(head)[2], preferred_element_type=jnp.float32)
        yield head, mixed / total, top, total


def fused(
    count,
    self_q,
    self_k,
    self_v,
    text_q,
    text_kv,
    text_len,
    self_out,
    text_back,
    stat_back,
    own_back,
    own,
    self_part,
    text_rows,
    context,
    text_part,
    text_full,
    inbound,
    joined,
    stat_part,
    stat_pack,
    stat_in,
    stat_join,
    stat_sum,
    live_len,
    query_recv,
    context_recv,
    inbound_recv,
    final_recv,
    sends,
    local_sem,
):
    me = lax.axis_index("seq")
    branch = lax.axis_index("enc")
    place, column = lax.div(me, COLUMNS), lax.rem(me, COLUMNS)
    half = lax.div(place, PLACES // HALVES)
    span = count // HALVES
    inner = lax.rem(place, 2) + half == 1
    outer = lax.rem(place, 2) + half != 1
    beside = COLUMNS * place + 1 - column
    near_place = place + 1 - 2 * lax.rem(place, 2)
    near, near_beside = COLUMNS * near_place + column, COLUMNS * near_place + 1 - column
    inner_there, outer_there = 2 - half, (PLACES - 1) * (1 - half)
    across = COLUMNS * inner_there + column
    there = (1 - half) * span
    rows = self_q.shape[1]
    query_total = count * rows
    context_rows = text_kv.shape[2]
    key_total = COLUMNS * context_rows
    self_span = own.shape[2]
    text_span = text_rows.shape[2]
    self_heads, text_heads = self_span // HEAD_DIM, text_span // HEAD_DIM
    chunk_heads = text_heads // CHUNKS
    chunk_span = chunk_heads * HEAD_DIM
    send_of = {name: sends.at[n] for name, n in SENDS.items()}

    def self_cols(device):
        return pl.ds(pl.multiple_of(device * self_span, self_span), self_span)

    def text_cols(side):
        return pl.ds(pl.multiple_of(side * text_span, text_span), text_span)

    def part_cols(side, chunk, width=1):
        return pl.ds(pl.multiple_of(side * text_span + chunk * chunk_span, chunk_span), width * chunk_span)

    def piece(chunk, width=1):
        return pl.ds(chunk * chunk_span, width * chunk_span)

    def remote(source, target, kind, recv, device):
        return pltpu.make_async_remote_copy(
            src_ref=source,
            dst_ref=target,
            send_sem=send_of[kind],
            recv_sem=recv,
            device_id={"seq": device},
            device_id_type=MESH,
        )

    def take(ref, sem):
        pltpu.make_async_copy(ref, ref, sem).wait()

    def start(copies):
        for copy in copies:
            copy.start()

    def mirror(bits):
        far_place = (
            place,
            near_place,
            lax.rem(place + 2, PLACES),
            PLACES - 1 - place,
        )[bits // 2]
        return COLUMNS * far_place + (column if bits % 2 == 0 else 1 - column)

    barrier = pltpu.get_barrier_semaphore()
    for step in range(1, count):
        pl.semaphore_signal(
            barrier, inc=1, device_id={"seq": lax.rem(me + step, count)}, device_id_type=MESH
        )
    kept_len = pltpu.make_async_copy(text_len, live_len, local_sem.at[3])
    kept_rows = pltpu.make_async_copy(text_q.at[0, :, text_cols(column)], text_rows.at[me], local_sem.at[0])
    kept_context = pltpu.make_async_copy(
        text_kv.at[0, :, :, text_cols(column)], context.at[column], local_sem.at[1]
    )
    kept_len.start()
    kept_rows.start()
    kept_context.start()
    for kind, source in enumerate((self_q, self_k, self_v)):
        pltpu.make_async_copy(
            source.at[0, :, self_cols(me)], own.at[kind * count + me], local_sem.at[2]
        ).start()

    with jax.named_scope("entry"):
        pl.semaphore_wait(barrier, count - 1)

    def held(origin, chunk):
        return text_rows.at[origin, :, piece(chunk)]

    def query_copy(kind, slot, chunk, source, origin, device):
        return remote(source, held(origin, chunk), kind, query_recv.at[slot, chunk], device)

    origins = [
        COLUMNS * inner_there + column,
        COLUMNS * outer_there + column,
        COLUMNS * inner_there + 1 - column,
        COLUMNS * outer_there + 1 - column,
    ]
    first = 2 + lax.rem(lax.rem(place, 2) + half + 1, 2)
    for chunk in range(CHUNKS):
        query_copy(
            "query", 0, chunk, text_q.at[0, :, part_cols(1 - column, chunk)], me, beside
        ).start()
    for chunk in range(CHUNKS):
        mine = text_q.at[0, :, part_cols(column, chunk)]
        query_copy("query", first, chunk, mine, me, across).start()
    for chunk in range(CHUNKS):
        mine = text_q.at[0, :, part_cols(column, chunk)]
        query_copy("query", 1, chunk, mine, me, near).start()
    def context_send(chunk):
        remote(
            text_kv.at[0, :, :, part_cols(1 - column, chunk)],
            context.at[column, :, :, piece(chunk)],
            "context",
            context_recv.at[chunk],
            beside,
        ).start()

    for chunk in range(CHUNKS):
        if chunk not in LATER:
            context_send(chunk)

    @pl.when(branch == 0)
    def _():
        for chunk in LATER:
            context_send(chunk)

    def start_self(bits):
        to = mirror(bits)
        for kind, source in enumerate((self_q, self_k, self_v)):
            remote(
                source.at[0, :, self_cols(to)], own.at[kind * count + me], "self", final_recv.at[3], to
            ).start()

    for mask, steps in ((outer, FIRST_OUTER), (inner, FIRST_INNER)):

        @pl.when(mask)
        def _(steps=steps):
            for step in steps:
                start_self(int(step[1:]))

    for chunk in range(CHUNKS):
        with jax.named_scope(f"q_beside{chunk}"):
            take(held(beside, chunk), query_recv.at[0, chunk])
        query_copy("query", first + 2, chunk, held(beside, chunk), beside, across).start()
        query_copy("query", 1, chunk, held(beside, chunk), beside, near).start()

    def far_waits(chunk):
        for n, origin in enumerate(origins):
            with jax.named_scope(f"q_far{chunk}{n}"):
                take(held(origin, chunk), query_recv.at[2 + n, chunk])
            yield n, origin

    kept_rows.wait()

    kept_len.wait()
    length = live_len[branch]
    live = place * key_total + lax.broadcasted_iota(jnp.int32, (1, key_total), 1) < length
    lane = lax.broadcasted_iota(jnp.int32, (query_total, HEAD_DIM), 1)
    short_lane = lax.broadcasted_iota(jnp.int32, (rows, HEAD_DIM), 1)

    def gathered():
        packed = jnp.zeros((rows, HEAD_DIM), jnp.float32)
        for n in range(span):
            moved = stat_part[there + n]
            if n:
                moved = pltpu.roll(moved, n * text_heads, 1)
            packed = jnp.where(lax.div(short_lane, text_heads) == n, moved, packed)
        return packed

    def inbound_half(chunk, later):
        return pl.ds(0, span) if chunk < CHUNKS - 1 else pl.ds(later * span // 2, span // 2)

    def join(chunk):
        with jax.named_scope(f"inb{chunk}"):
            take(stat_in.at[chunk], inbound_recv.at[1, chunk])
            take(inbound.at[inbound_half(chunk, 0), :, piece(chunk)], inbound_recv.at[0, chunk])
        sides = [gathered(), stat_in[chunk]]
        highest = jnp.maximum(*sides)
        shares = [jnp.exp2(side - highest) for side in sides]
        whole = shares[0] + shares[1]
        shares = [share / whole for share in shares]
        ours = lax.div(lax.rem(short_lane, text_heads), chunk_heads) == chunk
        final = jnp.where(ours, highest + jnp.log2(whole), stat_sum[...])
        stat_sum[...] = final
        for n in range(span):
            if chunk == CHUNKS - 1:
                stat_join[n] = pltpu.roll(final, HEAD_DIM - n * text_heads, 1) if n else final
                remote(
                    stat_join.at[n],
                    stat_back.at[HALVES, column],
                    "joined_stat",
                    final_recv.at[1],
                    there + n,
                ).start()
        for n in range(span):
            if chunk == CHUNKS - 1 and n == span // 2:
                take(inbound.at[inbound_half(chunk, 1), :, piece(chunk)], inbound_recv.at[0, chunk + 1])
            for head in range(chunk * chunk_heads, (chunk + 1) * chunk_heads):
                cols = slice(head * HEAD_DIM, (head + 1) * HEAD_DIM)
                at = n * text_heads + head
                merged = (
                    text_full[there + n, :, cols] * shares[0][:, at : at + 1]
                    + inbound[n, :, cols].astype(jnp.float32) * shares[1][:, at : at + 1]
                )
                joined[n, :, cols] = merged.astype(jnp.bfloat16)
            remote(
                joined.at[n, :, piece(chunk)],
                text_back.at[HALVES, :, part_cols(column, chunk)],
                "joined",
                final_recv.at[0],
                there + n,
            ).start()

    neighbours = ((0, beside), (1, near), (1, near_beside))

    def inbound_send(chunk, later):
        rows_of = inbound_half(chunk, later)
        remote(
            text_part.at[pl.ds(there + rows_of.start, rows_of.size), :, piece(chunk)],
            inbound.at[rows_of, :, piece(chunk)],
            "inbound",
            inbound_recv.at[0, chunk + later],
            near,
        ).start()

    def text_chunk(chunk, role):
        if role == "outer":
            for _n in far_waits(chunk):
                pass
        with jax.named_scope(f"q_near{chunk}"):
            take(text_rows.at[pl.ds(0, 2), :, piece(chunk)], query_recv.at[1, chunk])
        with jax.named_scope(f"kv{chunk}"):
            take(context.at[0, :, :, piece(chunk)], context_recv.at[chunk])
        tops, totals = jnp.full((query_total, HEAD_DIM), FAR, jnp.float32), 1.0

        def loads(head):
            cols = slice(head * HEAD_DIM, (head + 1) * HEAD_DIM)
            return (
                text_rows[:, :, cols].reshape(query_total, HEAD_DIM),
                context[:, 0, :, cols].reshape(key_total, HEAD_DIM),
                context[:, 1, :, cols].reshape(key_total, HEAD_DIM),
            )

        heads = range(chunk * chunk_heads, (chunk + 1) * chunk_heads)
        for head, mixed, top, total in attend(loads, heads, live):
            cols = slice(head * HEAD_DIM, (head + 1) * HEAD_DIM)
            share = mixed.reshape(count, rows, HEAD_DIM)
            text_full[:, :, cols] = share
            text_part[:, :, cols] = share.astype(jnp.bfloat16)
            tops = jnp.where(lane == head, top, tops)
            totals = jnp.where(lane == head, total, totals)
        if role == "outer":
            inbound_send(chunk, 0)
        levels = (tops * SCALE + jnp.log2(totals)).reshape(count, rows, HEAD_DIM)
        if chunk:
            before = lax.broadcasted_iota(jnp.int32, (1, 1, HEAD_DIM), 2) < chunk * chunk_heads
            levels = jnp.where(before, stat_part[...], levels)
        stat_part[...] = levels
        if role == "outer":
            stat_pack[chunk] = gathered()
            remote(
                stat_pack.at[chunk], stat_in.at[chunk], "inbound_stat", inbound_recv.at[1, chunk], near
            ).start()
            if chunk == CHUNKS - 1:
                inbound_send(chunk, 1)

    def near_send(low, high):
        for slot, device in neighbours:
            remote(
                text_part.at[device, :, piece(low, high + 1 - low)],
                text_back.at[slot, :, part_cols(column, low, high + 1 - low)],
                "near",
                final_recv.at[0],
                device,
            ).start()

    def near_stats():
        for slot, device in neighbours:
            remote(
                stat_part.at[device], stat_back.at[slot, column], "near_stat", final_recv.at[1], device
            ).start()

    def self_attention():
        take(own.at[pl.ds(0, 3)], local_sem.at[2])
        with jax.named_scope("self"):
            take(own.at[pl.ds(0, 3 * (count - 1))], final_recv.at[3])

        def loads(head):
            cols = slice(head * HEAD_DIM, (head + 1) * HEAD_DIM)
            return [
                own[kind * count : (kind + 1) * count, :, cols].reshape(query_total, HEAD_DIM)
                for kind in range(3)
            ]

        for head, mixed, _, _ in attend(loads, range(self_heads), None):
            cols = slice(head * HEAD_DIM, (head + 1) * HEAD_DIM)
            self_part[:, :, cols] = mixed.astype(jnp.bfloat16).reshape(count, rows, HEAD_DIM)
        for n in range(count - 1):
            to = n + lax.div(n + count - me, count)
            remote(
                self_part.at[to], self_out.at[0, :, self_cols(me)], "self_return", final_recv.at[2], to
            ).start()

    def relay():
        for chunk in range(CHUNKS):
            for n, origin in far_waits(chunk):
                query_copy("relay", 2 + n, chunk, held(origin, chunk), origin, near).start()

    def run(role, steps):
        for step in steps:
            name, _, only = step.partition(".")
            kind, digits = name[0], [int(digit) for digit in name[1:]]
            action = {
                "b": start_self,
                "x": context_send,
                "c": functools.partial(text_chunk, role=role),
                "n": near_send,
                "j": join,
                "r": relay,
                "t": near_stats,
                "s": self_attention,
            }[kind]
            if only:
                pl.when(branch == int(only))(functools.partial(action, *digits))
            else:
                action(*digits)

    kept_context.wait()

    @pl.when(outer)
    def _():
        run("outer", OUTER)

    @pl.when(inner)
    def _():
        stat_sum[...] = jnp.zeros_like(stat_sum)
        run("inner", INNER)

    kept_part = pltpu.make_async_copy(text_full.at[me], own_back, local_sem.at[0])
    kept_stat = pltpu.make_async_copy(stat_part.at[me], stat_back.at[0, column], local_sem.at[1])
    kept_self = pltpu.make_async_copy(self_part.at[me], self_out.at[0, :, self_cols(me)], local_sem.at[2])
    kept_part.start()
    kept_stat.start()
    kept_self.start()
    kept_part.wait()
    kept_stat.wait()
    kept_self.wait()
    with jax.named_scope("back"):
        take(text_part.at[pl.ds(0, 3 + COLUMNS)], final_recv.at[0])
    with jax.named_scope("back_stat"):
        take(stat_part.at[pl.ds(0, 3 + COLUMNS)], final_recv.at[1])
    with jax.named_scope("self_out"):
        take(self_part.at[pl.ds(0, count - 1)], final_recv.at[2])
    with jax.named_scope("sends"):
        take(text_full, sends.at[0])
        take(text_rows.at[pl.ds(0, count - 1)], sends.at[1])
        take(stat_part.at[pl.ds(0, count - 1)], sends.at[3])

    @pl.when(outer)
    def _():
        take(inbound, sends.at[2])

    @pl.when(inner)
    def _():
        take(text_rows, sends.at[2])


def settle(self_in, text_in, stat_in, own_in, self_out, text_out, mixed, out_sem):
    column = lax.rem(lax.axis_index("seq"), COLUMNS)
    text_span = own_in.shape[1]
    leaving = [pltpu.make_async_copy(self_in, self_out, out_sem.at[0])]
    leaving[0].start()
    for side in range(COLUMNS):
        sides = [stat_in[n, side] for n in range(HALVES + 1)]
        highest = functools.reduce(jnp.maximum, sides)
        shares = [jnp.exp2(each - highest) for each in sides]
        whole = sum(shares)
        shares = [share / whole for share in shares]
        for head in range(text_span // HEAD_DIM):
            cols = slice(side * text_span + head * HEAD_DIM, side * text_span + (head + 1) * HEAD_DIM)
            here = jnp.where(
                column == side,
                own_in[:, head * HEAD_DIM : (head + 1) * HEAD_DIM],
                text_in[0, :, cols].astype(jnp.float32),
            )
            merged = here * shares[0][:, head : head + 1] + sum(
                text_in[n, :, cols].astype(jnp.float32) * shares[n][:, head : head + 1]
                for n in range(1, HALVES + 1)
            )
            mixed[0, :, cols] = merged.astype(jnp.bfloat16)
        piece = pl.ds(side * text_span, text_span)
        leaving.append(
            pltpu.make_async_copy(mixed.at[:, :, piece], text_out.at[:, :, piece], out_sem.at[1 + side])
        )
        leaving[1 + side].start()
    for copy in leaving:
        copy.wait()


def fused_shards(self_queries, self_keys, self_values, text_queries, text_kv, text_len):
    count = lax.axis_size("seq")
    rows, channels = self_queries.shape[1:]
    context_rows = text_kv.shape[2]
    span = count // HALVES
    self_span, text_span = channels // count, channels // COLUMNS
    operands = (self_queries, self_keys, self_values, text_queries, text_kv, text_len)
    in_place = pl.BlockSpec(memory_space=pl.ANY)
    bf16, f32 = jnp.bfloat16, jnp.float32
    out = jax.ShapeDtypeStruct((1, rows, channels), bf16)
    dma = pltpu.SemaphoreType.DMA
    results = pl.pallas_call(
        functools.partial(fused, count),
        out_shape=(
            out,
            jax.ShapeDtypeStruct((HALVES + 1, rows, channels), bf16),
            jax.ShapeDtypeStruct((HALVES + 1, COLUMNS, rows, HEAD_DIM), f32),
            jax.ShapeDtypeStruct((rows, text_span), f32),
        ),
        in_specs=[in_place] * 6,
        out_specs=(in_place,) * 4,
        scratch_shapes=[
            pltpu.VMEM((3 * count, rows, self_span), bf16),
            pltpu.VMEM((count, rows, self_span), bf16),
            pltpu.VMEM((count, rows, text_span), bf16),
            pltpu.VMEM((COLUMNS, 2, context_rows, text_span), bf16),
            pltpu.VMEM((count, rows, text_span), bf16),
            pltpu.VMEM((count, rows, text_span), f32),
            pltpu.VMEM((span, rows, text_span), bf16),
            pltpu.VMEM((span, rows, text_span), bf16),
            pltpu.VMEM((count, rows, HEAD_DIM), f32),
            pltpu.VMEM((CHUNKS, rows, HEAD_DIM), f32),
            pltpu.VMEM((CHUNKS, rows, HEAD_DIM), f32),
            pltpu.VMEM((span, rows, HEAD_DIM), f32),
            pltpu.VMEM((rows, HEAD_DIM), f32),
            pltpu.SMEM(text_len.shape, jnp.int32),
            dma((2 + span, CHUNKS)),
            dma((CHUNKS,)),
            dma((2, CHUNKS + 1)),
            dma((4,)),
            dma((4,)),
            dma((4,)),
        ],
        compiler_params=pltpu.CompilerParams(
            collective_id=0, has_side_effects=True, vmem_limit_bytes=GRANT
        ),
        name="attention",
    )(*[pltpu.with_memory_space_constraint(each, pltpu.HBM) for each in operands])
    return pl.pallas_call(
        settle,
        out_shape=(out, out),
        in_specs=[pl.BlockSpec(memory_space=pltpu.VMEM)] * 4,
        out_specs=(in_place, in_place),
        scratch_shapes=[pltpu.VMEM((1, rows, channels), bf16), dma((1 + COLUMNS,))],
        compiler_params=pltpu.CompilerParams(vmem_limit_bytes=GRANT),
        name="settle",
    )(*results)


def solution(mesh):
    count = mesh.shape["seq"]
    fits = count == COLUMNS * PLACES and HEADS % count == 0
    return jax.shard_map(
        fused_shards if fits else shards,
        mesh=mesh,
        in_specs=(
            P("enc", ("groups", "seq"), None),
            P("enc", ("groups", "seq"), None),
            P("enc", ("groups", "seq"), None),
            P("enc", ("groups", "seq"), None),
            P("enc", None, ("groups", "seq"), None),
            P("groups"),
        ),
        out_specs=(P("enc", ("groups", "seq"), None), P("enc", ("groups", "seq"), None)),
        check_vma=False,
    )
```

```python
import functools
import math

import jax
import jax.numpy as jnp
from jax import lax
from jax.experimental import pallas as pl
from jax.experimental.pallas import tpu as pltpu
from jax.sharding import PartitionSpec as P

HEADS = 32
HEAD_DIM = 128


def absorb(run_state, queries, key_rows, value_rows, live_mask):
    running_max, row_total, weighted_sum = run_state
    scores = jnp.einsum(
        "qpd,kpd->pqk", queries, key_rows, preferred_element_type=jnp.float32
    ) / math.sqrt(HEAD_DIM)
    scores = jnp.where(live_mask[None, None, :], scores, -1e30)
    new_max = jnp.maximum(running_max, jnp.max(scores, axis=2))
    weights = jnp.where(live_mask[None, None, :], jnp.exp(scores - new_max[:, :, None]), 0.0)
    factor = jnp.exp(running_max - new_max)
    row_total = row_total * factor + jnp.sum(weights, axis=2)
    weighted_sum = weighted_sum * factor[:, :, None] + jnp.einsum(
        "pqk,kpd->pqd", weights.astype(jnp.bfloat16), value_rows, preferred_element_type=jnp.float32
    )
    return (new_max, row_total, weighted_sum)


def empty_state(head_count, query_count):
    return (
        jnp.full((head_count, query_count), -1e30, jnp.float32),
        jnp.zeros((head_count, query_count), jnp.float32),
        jnp.zeros((head_count, query_count, HEAD_DIM), jnp.float32),
    )


def finish(run_state):
    running_max, row_total, weighted_sum = run_state
    return (weighted_sum / row_total[:, :, None]).transpose(1, 0, 2).astype(jnp.bfloat16)


def block_attention(queries, key_rows, value_rows, live_mask):
    query_total, heads_here, head_width = queries.shape
    key_total = key_rows.shape[0]
    key_block = 1024 if key_total % 1024 == 0 else key_total
    query_block = 512 if query_total % 512 == 0 else query_total
    key_blocks = key_rows.reshape(key_total // key_block, key_block, heads_here, head_width)
    value_blocks = value_rows.reshape(key_total // key_block, key_block, heads_here, head_width)
    live_blocks = live_mask.reshape(key_total // key_block, key_block)

    def one_block(query_piece):

        def absorb_block(run_state, pieces):
            return (absorb(run_state, query_piece, pieces[0], pieces[1], pieces[2]), None)

        final_state, unused = lax.scan(
            absorb_block,
            empty_state(heads_here, query_block),
            (key_blocks, value_blocks, live_blocks),
        )
        return finish(final_state)

    blended = lax.map(
        one_block, queries.reshape(query_total // query_block, query_block, heads_here, head_width)
    )
    return blended.reshape(query_total, heads_here, head_width)


def shards(self_queries, self_keys, self_values, text_queries, text_kv, text_len):
    token_rows = self_queries.shape[1]
    channel_count = self_queries.shape[2]
    seq_count = lax.axis_size("seq")
    quarter_count = max(seq_count // HEADS, 1)
    heads_here = max(HEADS // seq_count, 1)
    group_count = HEADS // heads_here
    head_span = heads_here * HEAD_DIM
    share_rows = token_rows // quarter_count
    query_total = share_rows * seq_count
    branch = lax.axis_index("enc")
    length = lax.dynamic_index_in_dim(text_len, branch, 0, keepdims=False)

    def head_view(tensor):
        return tensor.reshape(1, share_rows, seq_count, head_span)

    def repeated(tensor):
        spread = jnp.broadcast_to(
            tensor.reshape(1, token_rows, 1, group_count, head_span),
            (1, token_rows, quarter_count, group_count, head_span),
        )
        return spread.reshape(1, token_rows, seq_count, head_span)

    head_queries, head_keys, head_values = (
        lax.all_to_all(head_view(self_queries), "seq", split_axis=2, concat_axis=1, tiled=True),
        lax.all_to_all(repeated(self_keys), "seq", split_axis=2, concat_axis=1, tiled=True),
        lax.all_to_all(repeated(self_values), "seq", split_axis=2, concat_axis=1, tiled=True),
    )
    key_rows = head_keys.reshape(-1, heads_here, HEAD_DIM)
    value_rows = head_values.reshape(-1, heads_here, HEAD_DIM)
    query_rows = head_queries.reshape(query_total, heads_here, HEAD_DIM)
    every_key = jnp.ones((key_rows.shape[0],), jnp.bool_)
    self_heads = block_attention(query_rows, key_rows, value_rows, every_key)
    head_text_queries = lax.all_to_all(
        head_view(text_queries), "seq", split_axis=2, concat_axis=1, tiled=True
    )
    context_rows = text_kv.shape[2]
    spread = jnp.broadcast_to(
        text_kv.reshape(1, 2, context_rows, 1, group_count, head_span),
        (1, 2, context_rows, quarter_count, group_count, head_span),
    )
    head_context = lax.all_to_all(
        spread.reshape(1, 2, context_rows, seq_count, head_span),
        "seq",
        split_axis=3,
        concat_axis=2,
        tiled=True,
    )
    text_total = head_context.shape[2]
    context_keys = head_context[0, 0].reshape(text_total, heads_here, HEAD_DIM)
    context_values = head_context[0, 1].reshape(text_total, heads_here, HEAD_DIM)
    live_mask = jnp.arange(text_total, dtype=jnp.int32) < length
    text_heads = block_attention(
        head_text_queries.reshape(query_total, heads_here, HEAD_DIM),
        context_keys,
        context_values,
        live_mask,
    )
    self_view = self_heads.reshape(1, seq_count, share_rows, 1, head_span)
    text_view = text_heads.reshape(1, seq_count, share_rows, 1, head_span)
    self_back, text_back = (
        lax.all_to_all(self_view, "seq", split_axis=1, concat_axis=3, tiled=True),
        lax.all_to_all(text_view, "seq", split_axis=1, concat_axis=3, tiled=True),
    )
    self_mixed = self_back.reshape(1, token_rows, channel_count)
    text_mixed = text_back.reshape(1, token_rows, channel_count)
    return (self_mixed, text_mixed)


COLUMNS = 2
HALVES = 2
PLACES = 4
CHUNKS = 4
GRANT = 12 * 1024 * 1024
SENDS = {"query": 0, "context": 0, "near": 0, "self": 1, "self_return": 1}
SENDS |= {"relay": 2, "joined": 2, "inbound": 2, "near_stat": 3, "inbound_stat": 3, "joined_stat": 3}
OUTER = ('b2.0', 'b2.1', 'b4.0', 'b6.1', 'c0', 'b6.0', 'b4.1', 'b7.0', 'b7.1', 'b5.0', 'b5.1', 'b3.1', 'b1.0', 'b1.1', 'b3.0', 'c1', 'c2', 'c3', 't.h0', 'n01.h0', 'n23.h0', 's', 'n01.h1', 'n23.h1', 't.h1')
INNER = ('b6', 'r', 'b2', 'b4.1', 'c0', 'b4.0', 'b7', 'b5', 'b3', 'b1', 'c1', 'n01.h0', 'c2', 'n22.h0', 'j0', 'c3', 't.h0', 'n33.h0', 'j1', 's', 'j2', 'j3', 'n01.h1', 'n23.h1', 't.h1')
FIRST_OUTER, FIRST_INNER = (), ()
LATER = tuple(sorted(int(step[1]) for step in OUTER if step[0] == "x"))
MESH = pl.DeviceIdType.MESH
FAR = -1e30
SCALE = math.log2(math.e) / math.sqrt(HEAD_DIM)


def attend(loads, heads, live):
    scores, sides = {}, {}
    for head in heads:
        queries, key_rows, _ = loads(head)
        scores[head] = lax.dot_general(
            queries, key_rows, (((1,), (1,)), ((), ())), preferred_element_type=jnp.float32
        )
    for head in heads:
        held = scores[head] if live is None else jnp.where(live, scores[head], FAR)
        top = jnp.max(held, axis=1, keepdims=True)
        weights = jnp.exp2((held - top) * SCALE)
        sides[head] = weights.astype(jnp.bfloat16), top, jnp.sum(weights, axis=1, keepdims=True)
    for head in heads:
        weights, top, total = sides[head]
        mixed = jnp.dot(weights, loads(head)[2], preferred_element_type=jnp.float32)
        yield head, mixed / total, top, total


def fused(
    count,
    self_q,
    self_k,
    self_v,
    text_q,
    text_kv,
    text_len,
    self_out,
    text_back,
    stat_back,
    own_back,
    own,
    self_part,
    text_rows,
    context,
    text_part,
    text_full,
    inbound,
    joined,
    stat_part,
    stat_pack,
    stat_in,
    stat_join,
    stat_sum,
    live_len,
    query_recv,
    context_recv,
    inbound_recv,
    final_recv,
    sends,
    local_sem,
):
    me = lax.axis_index("seq")
    branch = lax.axis_index("enc")
    place, column = lax.div(me, COLUMNS), lax.rem(me, COLUMNS)
    half = lax.div(place, PLACES // HALVES)
    span = count // HALVES
    inner = lax.rem(place, 2) + half == 1
    outer = lax.rem(place, 2) + half != 1
    beside = COLUMNS * place + 1 - column
    near_place = place + 1 - 2 * lax.rem(place, 2)
    near, near_beside = COLUMNS * near_place + column, COLUMNS * near_place + 1 - column
    inner_there, outer_there = 2 - half, (PLACES - 1) * (1 - half)
    across = COLUMNS * inner_there + column
    there = (1 - half) * span
    rows = self_q.shape[1]
    query_total = count * rows
    context_rows = text_kv.shape[2]
    key_total = COLUMNS * context_rows
    self_span = own.shape[2]
    text_span = text_rows.shape[2]
    self_heads, text_heads = self_span // HEAD_DIM, text_span // HEAD_DIM
    chunk_heads = text_heads // CHUNKS
    chunk_span = chunk_heads * HEAD_DIM
    send_of = {name: sends.at[n] for name, n in SENDS.items()}

    def self_cols(device):
        return pl.ds(pl.multiple_of(device * self_span, self_span), self_span)

    def text_cols(side):
        return pl.ds(pl.multiple_of(side * text_span, text_span), text_span)

    def part_cols(side, chunk, width=1):
        return pl.ds(pl.multiple_of(side * text_span + chunk * chunk_span, chunk_span), width * chunk_span)

    def piece(chunk, width=1):
        return pl.ds(chunk * chunk_span, width * chunk_span)

    def remote(source, target, kind, recv, device):
        return pltpu.make_async_remote_copy(
            src_ref=source,
            dst_ref=target,
            send_sem=send_of[kind],
            recv_sem=recv,
            device_id={"seq": device},
            device_id_type=MESH,
        )

    def take(ref, sem):
        pltpu.make_async_copy(ref, ref, sem).wait()

    def start(copies):
        for copy in copies:
            copy.start()

    def mirror(bits):
        far_place = (
            place,
            near_place,
            lax.rem(place + 2, PLACES),
            PLACES - 1 - place,
        )[bits // 2]
        return COLUMNS * far_place + (column if bits % 2 == 0 else 1 - column)

    barrier = pltpu.get_barrier_semaphore()
    for step in range(1, count):
        pl.semaphore_signal(
            barrier, inc=1, device_id={"seq": lax.rem(me + step, count)}, device_id_type=MESH
        )
    kept_len = pltpu.make_async_copy(text_len, live_len, local_sem.at[3])
    kept_rows = pltpu.make_async_copy(text_q.at[0, :, text_cols(column)], text_rows.at[me], local_sem.at[0])
    kept_context = pltpu.make_async_copy(
        text_kv.at[0, :, :, text_cols(column)], context.at[column], local_sem.at[1]
    )
    kept_len.start()
    kept_rows.start()
    kept_context.start()
    for kind, source in enumerate((self_q, self_k, self_v)):
        pltpu.make_async_copy(
            source.at[0, :, self_cols(me)], own.at[kind * count + me], local_sem.at[2]
        ).start()

    with jax.named_scope("entry"):
        pl.semaphore_wait(barrier, count - 1)

    def held(origin, chunk):
        return text_rows.at[origin, :, piece(chunk)]

    def query_copy(kind, slot, chunk, source, origin, device):
        return remote(source, held(origin, chunk), kind, query_recv.at[slot, chunk], device)

    origins = [
        COLUMNS * inner_there + column,
        COLUMNS * outer_there + column,
        COLUMNS * inner_there + 1 - column,
        COLUMNS * outer_there + 1 - column,
    ]
    first = 2 + lax.rem(lax.rem(place, 2) + half + 1, 2)
    for chunk in range(CHUNKS):
        query_copy(
            "query", 0, chunk, text_q.at[0, :, part_cols(1 - column, chunk)], me, beside
        ).start()
    for chunk in range(CHUNKS):
        mine = text_q.at[0, :, part_cols(column, chunk)]
        query_copy("query", first, chunk, mine, me, across).start()
    for chunk in range(CHUNKS):
        mine = text_q.at[0, :, part_cols(column, chunk)]
        query_copy("query", 1, chunk, mine, me, near).start()
    def context_send(chunk):
        remote(
            text_kv.at[0, :, :, part_cols(1 - column, chunk)],
            context.at[column, :, :, piece(chunk)],
            "context",
            context_recv.at[chunk],
            beside,
        ).start()

    for chunk in range(CHUNKS):
        if chunk not in LATER:
            context_send(chunk)

    @pl.when(branch == 0)
    def _():
        for chunk in LATER:
            context_send(chunk)

    def start_self(bits):
        to = mirror(bits)
        for kind, source in enumerate((self_q, self_k, self_v)):
            remote(
                source.at[0, :, self_cols(to)], own.at[kind * count + me], "self", final_recv.at[3], to
            ).start()

    for mask, steps in ((outer, FIRST_OUTER), (inner, FIRST_INNER)):

        @pl.when(mask)
        def _(steps=steps):
            for step in steps:
                start_self(int(step[1:]))

    for chunk in range(CHUNKS):
        with jax.named_scope(f"q_beside{chunk}"):
            take(held(beside, chunk), query_recv.at[0, chunk])
        query_copy("query", first + 2, chunk, held(beside, chunk), beside, across).start()
        query_copy("query", 1, chunk, held(beside, chunk), beside, near).start()

    def far_waits(chunk):
        for n, origin in enumerate(origins):
            with jax.named_scope(f"q_far{chunk}{n}"):
                take(held(origin, chunk), query_recv.at[2 + n, chunk])
            yield n, origin

    kept_rows.wait()

    kept_len.wait()
    length = live_len[branch]
    live = place * key_total + lax.broadcasted_iota(jnp.int32, (1, key_total), 1) < length
    lane = lax.broadcasted_iota(jnp.int32, (query_total, HEAD_DIM), 1)
    short_lane = lax.broadcasted_iota(jnp.int32, (rows, HEAD_DIM), 1)

    def gathered():
        packed = jnp.zeros((rows, HEAD_DIM), jnp.float32)
        for n in range(span):
            moved = stat_part[there + n]
            if n:
                moved = pltpu.roll(moved, n * text_heads, 1)
            packed = jnp.where(lax.div(short_lane, text_heads) == n, moved, packed)
        return packed

    def inbound_half(chunk, later):
        return pl.ds(0, span) if chunk < CHUNKS - 1 else pl.ds(later * span // 2, span // 2)

    def join(chunk):
        with jax.named_scope(f"inb{chunk}"):
            take(stat_in.at[chunk], inbound_recv.at[1, chunk])
            take(inbound.at[inbound_half(chunk, 0), :, piece(chunk)], inbound_recv.at[0, chunk])
        sides = [gathered(), stat_in[chunk]]
        highest = jnp.maximum(*sides)
        shares = [jnp.exp2(side - highest) for side in sides]
        whole = shares[0] + shares[1]
        shares = [share / whole for share in shares]
        ours = lax.div(lax.rem(short_lane, text_heads), chunk_heads) == chunk
        final = jnp.where(ours, highest + jnp.log2(whole), stat_sum[...])
        stat_sum[...] = final
        for n in range(span):
            if chunk == CHUNKS - 1:
                stat_join[n] = pltpu.roll(final, HEAD_DIM - n * text_heads, 1) if n else final
                remote(
                    stat_join.at[n],
                    stat_back.at[HALVES, column],
                    "joined_stat",
                    final_recv.at[1],
                    there + n,
                ).start()
        for n in range(span):
            if chunk == CHUNKS - 1 and n == span // 2:
                take(inbound.at[inbound_half(chunk, 1), :, piece(chunk)], inbound_recv.at[0, chunk + 1])
            for head in range(chunk * chunk_heads, (chunk + 1) * chunk_heads):
                cols = slice(head * HEAD_DIM, (head + 1) * HEAD_DIM)
                at = n * text_heads + head
                merged = (
                    text_full[there + n, :, cols] * shares[0][:, at : at + 1]
                    + inbound[n, :, cols].astype(jnp.float32) * shares[1][:, at : at + 1]
                )
                joined[n, :, cols] = merged.astype(jnp.bfloat16)
            remote(
                joined.at[n, :, piece(chunk)],
                text_back.at[HALVES, :, part_cols(column, chunk)],
                "joined",
                final_recv.at[0],
                there + n,
            ).start()

    neighbours = (
        *((1, COLUMNS * near_place + side) for side in range(COLUMNS)),
        (0, beside),
    )

    def inbound_send(chunk, later):
        rows_of = inbound_half(chunk, later)
        remote(
            text_part.at[pl.ds(there + rows_of.start, rows_of.size), :, piece(chunk)],
            inbound.at[rows_of, :, piece(chunk)],
            "inbound",
            inbound_recv.at[0, chunk + later],
            near,
        ).start()

    def text_chunk(chunk, role):
        if role == "outer":
            for _n in far_waits(chunk):
                pass
        with jax.named_scope(f"q_near{chunk}"):
            take(text_rows.at[pl.ds(0, 2), :, piece(chunk)], query_recv.at[1, chunk])
        with jax.named_scope(f"kv{chunk}"):
            take(context.at[0, :, :, piece(chunk)], context_recv.at[chunk])
        tops, totals = jnp.full((query_total, HEAD_DIM), FAR, jnp.float32), 1.0

        def loads(head):
            cols = slice(head * HEAD_DIM, (head + 1) * HEAD_DIM)
            return (
                text_rows[:, :, cols].reshape(query_total, HEAD_DIM),
                context[:, 0, :, cols].reshape(key_total, HEAD_DIM),
                context[:, 1, :, cols].reshape(key_total, HEAD_DIM),
            )

        heads = range(chunk * chunk_heads, (chunk + 1) * chunk_heads)
        for head, mixed, top, total in attend(loads, heads, live):
            cols = slice(head * HEAD_DIM, (head + 1) * HEAD_DIM)
            share = mixed.reshape(count, rows, HEAD_DIM)
            text_full[:, :, cols] = share
            text_part[:, :, cols] = share.astype(jnp.bfloat16)
            tops = jnp.where(lane == head, top, tops)
            totals = jnp.where(lane == head, total, totals)
        if role == "outer":
            inbound_send(chunk, 0)
        levels = (tops * SCALE + jnp.log2(totals)).reshape(count, rows, HEAD_DIM)
        if chunk:
            before = lax.broadcasted_iota(jnp.int32, (1, 1, HEAD_DIM), 2) < chunk * chunk_heads
            levels = jnp.where(before, stat_part[...], levels)
        stat_part[...] = levels
        if role == "outer":
            stat_pack[chunk] = gathered()
            remote(
                stat_pack.at[chunk], stat_in.at[chunk], "inbound_stat", inbound_recv.at[1, chunk], near
            ).start()
            if chunk == CHUNKS - 1:
                inbound_send(chunk, 1)

    def near_send(low, high):
        for slot, device in neighbours:
            remote(
                text_part.at[device, :, piece(low, high + 1 - low)],
                text_back.at[slot, :, part_cols(column, low, high + 1 - low)],
                "near",
                final_recv.at[0],
                device,
            ).start()

    def near_stats():
        for slot, device in neighbours:
            remote(
                stat_part.at[device], stat_back.at[slot, column], "near_stat", final_recv.at[1], device
            ).start()

    def self_attention():
        take(own.at[pl.ds(0, 3)], local_sem.at[2])
        with jax.named_scope("self"):
            take(own.at[pl.ds(0, 3 * (count - 1))], final_recv.at[3])

        def loads(head):
            cols = slice(head * HEAD_DIM, (head + 1) * HEAD_DIM)
            return [
                own[kind * count : (kind + 1) * count, :, cols].reshape(query_total, HEAD_DIM)
                for kind in range(3)
            ]

        for head, mixed, _, _ in attend(loads, range(self_heads), None):
            cols = slice(head * HEAD_DIM, (head + 1) * HEAD_DIM)
            self_part[:, :, cols] = mixed.astype(jnp.bfloat16).reshape(count, rows, HEAD_DIM)
        for n in range(count - 1):
            to = n + lax.div(n + count - me, count)
            remote(
                self_part.at[to], self_out.at[0, :, self_cols(me)], "self_return", final_recv.at[2], to
            ).start()

    def relay():
        for chunk in range(CHUNKS):
            for n, origin in far_waits(chunk):
                query_copy("relay", 2 + n, chunk, held(origin, chunk), origin, near).start()

    def run(role, steps):
        for step in steps:
            name, _, only = step.partition(".")
            kind, digits = name[0], [int(digit) for digit in name[1:]]
            action = {
                "b": start_self,
                "x": context_send,
                "c": functools.partial(text_chunk, role=role),
                "n": near_send,
                "j": join,
                "r": relay,
                "t": near_stats,
                "s": self_attention,
            }[kind]
            if only:
                holds = half == int(only[1:]) if only[0] == "h" else branch == int(only)
                pl.when(holds)(functools.partial(action, *digits))
            else:
                action(*digits)

    kept_context.wait()

    @pl.when(outer)
    def _():
        run("outer", OUTER)

    @pl.when(inner)
    def _():
        stat_sum[...] = jnp.zeros_like(stat_sum)
        run("inner", INNER)

    kept_part = pltpu.make_async_copy(text_full.at[me], own_back, local_sem.at[0])
    kept_stat = pltpu.make_async_copy(stat_part.at[me], stat_back.at[0, column], local_sem.at[1])
    kept_self = pltpu.make_async_copy(self_part.at[me], self_out.at[0, :, self_cols(me)], local_sem.at[2])
    kept_part.start()
    kept_stat.start()
    kept_self.start()
    kept_part.wait()
    kept_stat.wait()
    kept_self.wait()
    with jax.named_scope("back"):
        take(text_part.at[pl.ds(0, 3 + COLUMNS)], final_recv.at[0])
    with jax.named_scope("back_stat"):
        take(stat_part.at[pl.ds(0, 3 + COLUMNS)], final_recv.at[1])
    with jax.named_scope("self_out"):
        take(self_part.at[pl.ds(0, count - 1)], final_recv.at[2])
    with jax.named_scope("sends"):
        take(text_full, sends.at[0])
        take(text_rows.at[pl.ds(0, count - 1)], sends.at[1])
        take(stat_part.at[pl.ds(0, count - 1)], sends.at[3])

    @pl.when(outer)
    def _():
        take(inbound, sends.at[2])

    @pl.when(inner)
    def _():
        take(text_rows, sends.at[2])


def settle(self_in, text_in, stat_in, own_in, self_out, text_out, mixed, out_sem):
    column = lax.rem(lax.axis_index("seq"), COLUMNS)
    text_span = own_in.shape[1]
    leaving = [pltpu.make_async_copy(self_in, self_out, out_sem.at[0])]
    leaving[0].start()
    for side in range(COLUMNS):
        sides = [stat_in[n, side] for n in range(HALVES + 1)]
        highest = functools.reduce(jnp.maximum, sides)
        shares = [jnp.exp2(each - highest) for each in sides]
        whole = sum(shares)
        shares = [share / whole for share in shares]
        for head in range(text_span // HEAD_DIM):
            cols = slice(side * text_span + head * HEAD_DIM, side * text_span + (head + 1) * HEAD_DIM)
            here = jnp.where(
                column == side,
                own_in[:, head * HEAD_DIM : (head + 1) * HEAD_DIM],
                text_in[0, :, cols].astype(jnp.float32),
            )
            merged = here * shares[0][:, head : head + 1] + sum(
                text_in[n, :, cols].astype(jnp.float32) * shares[n][:, head : head + 1]
                for n in range(1, HALVES + 1)
            )
            mixed[0, :, cols] = merged.astype(jnp.bfloat16)
        piece = pl.ds(side * text_span, text_span)
        leaving.append(
            pltpu.make_async_copy(mixed.at[:, :, piece], text_out.at[:, :, piece], out_sem.at[1 + side])
        )
        leaving[1 + side].start()
    for copy in leaving:
        copy.wait()


def fused_shards(self_queries, self_keys, self_values, text_queries, text_kv, text_len):
    count = lax.axis_size("seq")
    rows, channels = self_queries.shape[1:]
    context_rows = text_kv.shape[2]
    span = count // HALVES
    self_span, text_span = channels // count, channels // COLUMNS
    operands = (self_queries, self_keys, self_values, text_queries, text_kv, text_len)
    in_place = pl.BlockSpec(memory_space=pl.ANY)
    bf16, f32 = jnp.bfloat16, jnp.float32
    out = jax.ShapeDtypeStruct((1, rows, channels), bf16)
    dma = pltpu.SemaphoreType.DMA
    results = pl.pallas_call(
        functools.partial(fused, count),
        out_shape=(
            out,
            jax.ShapeDtypeStruct((HALVES + 1, rows, channels), bf16),
            jax.ShapeDtypeStruct((HALVES + 1, COLUMNS, rows, HEAD_DIM), f32),
            jax.ShapeDtypeStruct((rows, text_span), f32),
        ),
        in_specs=[in_place] * 6,
        out_specs=(in_place,) * 4,
        scratch_shapes=[
            pltpu.VMEM((3 * count, rows, self_span), bf16),
            pltpu.VMEM((count, rows, self_span), bf16),
            pltpu.VMEM((count, rows, text_span), bf16),
            pltpu.VMEM((COLUMNS, 2, context_rows, text_span), bf16),
            pltpu.VMEM((count, rows, text_span), bf16),
            pltpu.VMEM((count, rows, text_span), f32),
            pltpu.VMEM((span, rows, text_span), bf16),
            pltpu.VMEM((span, rows, text_span), bf16),
            pltpu.VMEM((count, rows, HEAD_DIM), f32),
            pltpu.VMEM((CHUNKS, rows, HEAD_DIM), f32),
            pltpu.VMEM((CHUNKS, rows, HEAD_DIM), f32),
            pltpu.VMEM((span, rows, HEAD_DIM), f32),
            pltpu.VMEM((rows, HEAD_DIM), f32),
            pltpu.SMEM(text_len.shape, jnp.int32),
            dma((2 + span, CHUNKS)),
            dma((CHUNKS,)),
            dma((2, CHUNKS + 1)),
            dma((4,)),
            dma((4,)),
            dma((4,)),
        ],
        compiler_params=pltpu.CompilerParams(
            collective_id=0, has_side_effects=True, vmem_limit_bytes=GRANT
        ),
        name="attention",
    )(*[pltpu.with_memory_space_constraint(each, pltpu.HBM) for each in operands])
    return pl.pallas_call(
        settle,
        out_shape=(out, out),
        in_specs=[pl.BlockSpec(memory_space=pltpu.VMEM)] * 4,
        out_specs=(in_place, in_place),
        scratch_shapes=[pltpu.VMEM((1, rows, channels), bf16), dma((1 + COLUMNS,))],
        compiler_params=pltpu.CompilerParams(vmem_limit_bytes=GRANT),
        name="settle",
    )(*results)


def solution(mesh):
    count = mesh.shape["seq"]
    fits = count == COLUMNS * PLACES and HEADS % count == 0
    return jax.shard_map(
        fused_shards if fits else shards,
        mesh=mesh,
        in_specs=(
            P("enc", ("groups", "seq"), None),
            P("enc", ("groups", "seq"), None),
            P("enc", ("groups", "seq"), None),
            P("enc", ("groups", "seq"), None),
            P("enc", None, ("groups", "seq"), None),
            P("groups"),
        ),
        out_specs=(P("enc", ("groups", "seq"), None), P("enc", ("groups", "seq"), None)),
        check_vma=False,
    )
```

```python
import functools
import math

import jax
import jax.numpy as jnp
from jax import lax
from jax.experimental import pallas as pl
from jax.experimental.pallas import tpu as pltpu
from jax.sharding import PartitionSpec as P

HEADS = 32
HEAD_DIM = 128


def absorb(run_state, queries, key_rows, value_rows, live_mask):
    running_max, row_total, weighted_sum = run_state
    scores = jnp.einsum(
        "qpd,kpd->pqk", queries, key_rows, preferred_element_type=jnp.float32
    ) / math.sqrt(HEAD_DIM)
    scores = jnp.where(live_mask[None, None, :], scores, -1e30)
    new_max = jnp.maximum(running_max, jnp.max(scores, axis=2))
    weights = jnp.where(live_mask[None, None, :], jnp.exp(scores - new_max[:, :, None]), 0.0)
    factor = jnp.exp(running_max - new_max)
    row_total = row_total * factor + jnp.sum(weights, axis=2)
    weighted_sum = weighted_sum * factor[:, :, None] + jnp.einsum(
        "pqk,kpd->pqd", weights.astype(jnp.bfloat16), value_rows, preferred_element_type=jnp.float32
    )
    return (new_max, row_total, weighted_sum)


def empty_state(head_count, query_count):
    return (
        jnp.full((head_count, query_count), -1e30, jnp.float32),
        jnp.zeros((head_count, query_count), jnp.float32),
        jnp.zeros((head_count, query_count, HEAD_DIM), jnp.float32),
    )


def finish(run_state):
    running_max, row_total, weighted_sum = run_state
    return (weighted_sum / row_total[:, :, None]).transpose(1, 0, 2).astype(jnp.bfloat16)


def block_attention(queries, key_rows, value_rows, live_mask):
    query_total, heads_here, head_width = queries.shape
    key_total = key_rows.shape[0]
    key_block = 1024 if key_total % 1024 == 0 else key_total
    query_block = 512 if query_total % 512 == 0 else query_total
    key_blocks = key_rows.reshape(key_total // key_block, key_block, heads_here, head_width)
    value_blocks = value_rows.reshape(key_total // key_block, key_block, heads_here, head_width)
    live_blocks = live_mask.reshape(key_total // key_block, key_block)

    def one_block(query_piece):

        def absorb_block(run_state, pieces):
            return (absorb(run_state, query_piece, pieces[0], pieces[1], pieces[2]), None)

        final_state, unused = lax.scan(
            absorb_block,
            empty_state(heads_here, query_block),
            (key_blocks, value_blocks, live_blocks),
        )
        return finish(final_state)

    blended = lax.map(
        one_block, queries.reshape(query_total // query_block, query_block, heads_here, head_width)
    )
    return blended.reshape(query_total, heads_here, head_width)


def shards(self_queries, self_keys, self_values, text_queries, text_kv, text_len):
    token_rows = self_queries.shape[1]
    channel_count = self_queries.shape[2]
    seq_count = lax.axis_size("seq")
    quarter_count = max(seq_count // HEADS, 1)
    heads_here = max(HEADS // seq_count, 1)
    group_count = HEADS // heads_here
    head_span = heads_here * HEAD_DIM
    share_rows = token_rows // quarter_count
    query_total = share_rows * seq_count
    branch = lax.axis_index("enc")
    length = lax.dynamic_index_in_dim(text_len, branch, 0, keepdims=False)

    def head_view(tensor):
        return tensor.reshape(1, share_rows, seq_count, head_span)

    def repeated(tensor):
        spread = jnp.broadcast_to(
            tensor.reshape(1, token_rows, 1, group_count, head_span),
            (1, token_rows, quarter_count, group_count, head_span),
        )
        return spread.reshape(1, token_rows, seq_count, head_span)

    head_queries, head_keys, head_values = (
        lax.all_to_all(head_view(self_queries), "seq", split_axis=2, concat_axis=1, tiled=True),
        lax.all_to_all(repeated(self_keys), "seq", split_axis=2, concat_axis=1, tiled=True),
        lax.all_to_all(repeated(self_values), "seq", split_axis=2, concat_axis=1, tiled=True),
    )
    key_rows = head_keys.reshape(-1, heads_here, HEAD_DIM)
    value_rows = head_values.reshape(-1, heads_here, HEAD_DIM)
    query_rows = head_queries.reshape(query_total, heads_here, HEAD_DIM)
    every_key = jnp.ones((key_rows.shape[0],), jnp.bool_)
    self_heads = block_attention(query_rows, key_rows, value_rows, every_key)
    head_text_queries = lax.all_to_all(
        head_view(text_queries), "seq", split_axis=2, concat_axis=1, tiled=True
    )
    context_rows = text_kv.shape[2]
    spread = jnp.broadcast_to(
        text_kv.reshape(1, 2, context_rows, 1, group_count, head_span),
        (1, 2, context_rows, quarter_count, group_count, head_span),
    )
    head_context = lax.all_to_all(
        spread.reshape(1, 2, context_rows, seq_count, head_span),
        "seq",
        split_axis=3,
        concat_axis=2,
        tiled=True,
    )
    text_total = head_context.shape[2]
    context_keys = head_context[0, 0].reshape(text_total, heads_here, HEAD_DIM)
    context_values = head_context[0, 1].reshape(text_total, heads_here, HEAD_DIM)
    live_mask = jnp.arange(text_total, dtype=jnp.int32) < length
    text_heads = block_attention(
        head_text_queries.reshape(query_total, heads_here, HEAD_DIM),
        context_keys,
        context_values,
        live_mask,
    )
    self_view = self_heads.reshape(1, seq_count, share_rows, 1, head_span)
    text_view = text_heads.reshape(1, seq_count, share_rows, 1, head_span)
    self_back, text_back = (
        lax.all_to_all(self_view, "seq", split_axis=1, concat_axis=3, tiled=True),
        lax.all_to_all(text_view, "seq", split_axis=1, concat_axis=3, tiled=True),
    )
    self_mixed = self_back.reshape(1, token_rows, channel_count)
    text_mixed = text_back.reshape(1, token_rows, channel_count)
    return (self_mixed, text_mixed)


COLUMNS = 2
HALVES = 2
PLACES = 4
CHUNKS = 4
GRANT = 12 * 1024 * 1024
SENDS = {"query": 0, "context": 0, "near": 0, "self": 1, "self_return": 1}
SENDS |= {"relay": 2, "joined": 2, "inbound": 2, "near_stat": 3, "inbound_stat": 3, "joined_stat": 3}
OUTER = ('b2.0', 'b2.1', 'b4.0', 'b6.1', 'c0', 'b6.0', 'b4.1', 'b7.0', 'b7.1', 'b5.0', 'b5.1', 'b3.1', 'b1.0', 'b1.1', 'b3.0', 'c1', 'c2', 'c3', 't.h0', 'n01.h0', 'n23.h0', 's', 'n01.h1', 'n23.h1', 't.h1')
INNER = ('b6', 'r', 'b2', 'b4.1', 'c0', 'b4.0', 'b7', 'b5', 'b3', 'b1', 'c1', 'n01.h0', 'c2', 'n22.h0', 'j0', 'c3', 't.h0', 'n33.h0', 'j1', 's', 'j2', 'j3', 'n01.h1', 'n23.h1', 't.h1')
FIRST_OUTER, FIRST_INNER = (), ()
LATER = tuple(sorted(int(step[1]) for step in OUTER if step[0] == "x"))
MESH = pl.DeviceIdType.MESH
FAR = -1e30
SCALE = math.log2(math.e) / math.sqrt(HEAD_DIM)


def attend(loads, heads, live):
    scores, sides = {}, {}
    for head in heads:
        queries, key_rows, _ = loads(head)
        scores[head] = lax.dot_general(
            queries, key_rows, (((1,), (1,)), ((), ())), preferred_element_type=jnp.float32
        )
    for head in heads:
        held = scores[head] if live is None else jnp.where(live, scores[head], FAR)
        top = jnp.max(held, axis=1, keepdims=True)
        weights = jnp.exp2((held - top) * SCALE)
        sides[head] = weights.astype(jnp.bfloat16), top, jnp.sum(weights, axis=1, keepdims=True)
    for head in heads:
        weights, top, total = sides[head]
        mixed = jnp.dot(weights, loads(head)[2], preferred_element_type=jnp.float32)
        yield head, mixed / total, top, total


def fused(
    count,
    self_q,
    self_k,
    self_v,
    text_q,
    text_kv,
    text_len,
    self_out,
    text_back,
    stat_back,
    own_back,
    own,
    self_part,
    text_rows,
    context,
    text_part,
    text_full,
    inbound,
    joined,
    stat_part,
    stat_pack,
    stat_in,
    stat_join,
    stat_sum,
    live_len,
    query_recv,
    context_recv,
    inbound_recv,
    final_recv,
    sends,
    local_sem,
):
    me = lax.axis_index("seq")
    branch = lax.axis_index("enc")
    place, column = lax.div(me, COLUMNS), lax.rem(me, COLUMNS)
    half = lax.div(place, PLACES // HALVES)
    span = count // HALVES
    inner = lax.rem(place, 2) + half == 1
    outer = lax.rem(place, 2) + half != 1
    beside = COLUMNS * place + 1 - column
    near_place = place + 1 - 2 * lax.rem(place, 2)
    near, near_beside = COLUMNS * near_place + column, COLUMNS * near_place + 1 - column
    inner_there, outer_there = 2 - half, (PLACES - 1) * (1 - half)
    across = COLUMNS * inner_there + column
    there = (1 - half) * span
    rows = self_q.shape[1]
    query_total = count * rows
    context_rows = text_kv.shape[2]
    key_total = COLUMNS * context_rows
    self_span = own.shape[2]
    text_span = text_rows.shape[2]
    self_heads, text_heads = self_span // HEAD_DIM, text_span // HEAD_DIM
    chunk_heads = text_heads // CHUNKS
    chunk_span = chunk_heads * HEAD_DIM
    send_of = {name: sends.at[n] for name, n in SENDS.items()}

    def self_cols(device):
        return pl.ds(pl.multiple_of(device * self_span, self_span), self_span)

    def text_cols(side):
        return pl.ds(pl.multiple_of(side * text_span, text_span), text_span)

    def part_cols(side, chunk, width=1):
        return pl.ds(pl.multiple_of(side * text_span + chunk * chunk_span, chunk_span), width * chunk_span)

    def piece(chunk, width=1):
        return pl.ds(chunk * chunk_span, width * chunk_span)

    def remote(source, target, kind, recv, device):
        return pltpu.make_async_remote_copy(
            src_ref=source,
            dst_ref=target,
            send_sem=send_of[kind],
            recv_sem=recv,
            device_id={"seq": device},
            device_id_type=MESH,
        )

    def take(ref, sem):
        pltpu.make_async_copy(ref, ref, sem).wait()

    def start(copies):
        for copy in copies:
            copy.start()

    def mirror(bits):
        far_place = (
            place,
            near_place,
            lax.rem(place + 2, PLACES),
            PLACES - 1 - place,
        )[bits // 2]
        return COLUMNS * far_place + (column if bits % 2 == 0 else 1 - column)

    barrier = pltpu.get_barrier_semaphore()
    for step in range(1, count):
        pl.semaphore_signal(
            barrier, inc=1, device_id={"seq": lax.rem(me + step, count)}, device_id_type=MESH
        )
    with jax.named_scope("entry"):
        pl.semaphore_wait(barrier, count - 1)

    def held(origin, chunk):
        return text_rows.at[origin, :, piece(chunk)]

    def query_copy(kind, slot, chunk, source, origin, device):
        return remote(source, held(origin, chunk), kind, query_recv.at[slot, chunk], device)

    origins = [
        COLUMNS * inner_there + column,
        COLUMNS * outer_there + column,
        COLUMNS * inner_there + 1 - column,
        COLUMNS * outer_there + 1 - column,
    ]
    first = 2 + lax.rem(lax.rem(place, 2) + half + 1, 2)
    for chunk in range(CHUNKS):
        query_copy(
            "query", 0, chunk, text_q.at[0, :, part_cols(1 - column, chunk)], me, beside
        ).start()
    for chunk in range(CHUNKS):
        mine = text_q.at[0, :, part_cols(column, chunk)]
        query_copy("query", first, chunk, mine, me, across).start()
    for chunk in range(CHUNKS):
        mine = text_q.at[0, :, part_cols(column, chunk)]
        query_copy("query", 1, chunk, mine, me, near).start()
    def context_send(chunk):
        remote(
            text_kv.at[0, :, :, part_cols(1 - column, chunk)],
            context.at[column, :, :, piece(chunk)],
            "context",
            context_recv.at[chunk],
            beside,
        ).start()

    for chunk in range(CHUNKS):
        if chunk not in LATER:
            context_send(chunk)

    @pl.when(branch == 0)
    def _():
        for chunk in LATER:
            context_send(chunk)

    kept_len = pltpu.make_async_copy(text_len, live_len, local_sem.at[3])
    kept_rows = pltpu.make_async_copy(text_q.at[0, :, text_cols(column)], text_rows.at[me], local_sem.at[0])
    kept_context = pltpu.make_async_copy(
        text_kv.at[0, :, :, text_cols(column)], context.at[column], local_sem.at[1]
    )
    kept_len.start()
    kept_rows.start()
    kept_context.start()
    for kind, source in enumerate((self_q, self_k, self_v)):
        pltpu.make_async_copy(
            source.at[0, :, self_cols(me)], own.at[kind * count + me], local_sem.at[2]
        ).start()

    def start_self(bits):
        to = mirror(bits)
        for kind, source in enumerate((self_q, self_k, self_v)):
            remote(
                source.at[0, :, self_cols(to)], own.at[kind * count + me], "self", final_recv.at[3], to
            ).start()

    for mask, steps in ((outer, FIRST_OUTER), (inner, FIRST_INNER)):

        @pl.when(mask)
        def _(steps=steps):
            for step in steps:
                start_self(int(step[1:]))

    for chunk in range(CHUNKS):
        with jax.named_scope(f"q_beside{chunk}"):
            take(held(beside, chunk), query_recv.at[0, chunk])
        query_copy("query", first + 2, chunk, held(beside, chunk), beside, across).start()
        query_copy("query", 1, chunk, held(beside, chunk), beside, near).start()

    def far_waits(chunk):
        for n, origin in enumerate(origins):
            with jax.named_scope(f"q_far{chunk}{n}"):
                take(held(origin, chunk), query_recv.at[2 + n, chunk])
            yield n, origin

    kept_rows.wait()

    kept_len.wait()
    length = live_len[branch]
    live = place * key_total + lax.broadcasted_iota(jnp.int32, (1, key_total), 1) < length
    lane = lax.broadcasted_iota(jnp.int32, (query_total, HEAD_DIM), 1)
    short_lane = lax.broadcasted_iota(jnp.int32, (rows, HEAD_DIM), 1)

    def gathered():
        packed = jnp.zeros((rows, HEAD_DIM), jnp.float32)
        for n in range(span):
            moved = stat_part[there + n]
            if n:
                moved = pltpu.roll(moved, n * text_heads, 1)
            packed = jnp.where(lax.div(short_lane, text_heads) == n, moved, packed)
        return packed

    def inbound_half(chunk, later):
        return pl.ds(0, span) if chunk < CHUNKS - 1 else pl.ds(later * span // 2, span // 2)

    def join(chunk):
        with jax.named_scope(f"inb{chunk}"):
            take(stat_in.at[chunk], inbound_recv.at[1, chunk])
            take(inbound.at[inbound_half(chunk, 0), :, piece(chunk)], inbound_recv.at[0, chunk])
        sides = [gathered(), stat_in[chunk]]
        highest = jnp.maximum(*sides)
        shares = [jnp.exp2(side - highest) for side in sides]
        whole = shares[0] + shares[1]
        shares = [share / whole for share in shares]
        ours = lax.div(lax.rem(short_lane, text_heads), chunk_heads) == chunk
        final = jnp.where(ours, highest + jnp.log2(whole), stat_sum[...])
        stat_sum[...] = final
        for n in range(span):
            if chunk == CHUNKS - 1:
                stat_join[n] = pltpu.roll(final, HEAD_DIM - n * text_heads, 1) if n else final
                remote(
                    stat_join.at[n],
                    stat_back.at[HALVES, column],
                    "joined_stat",
                    final_recv.at[1],
                    there + n,
                ).start()
        for n in range(span):
            if chunk == CHUNKS - 1 and n == span // 2:
                take(inbound.at[inbound_half(chunk, 1), :, piece(chunk)], inbound_recv.at[0, chunk + 1])
            for head in range(chunk * chunk_heads, (chunk + 1) * chunk_heads):
                cols = slice(head * HEAD_DIM, (head + 1) * HEAD_DIM)
                at = n * text_heads + head
                merged = (
                    text_full[there + n, :, cols] * shares[0][:, at : at + 1]
                    + inbound[n, :, cols].astype(jnp.float32) * shares[1][:, at : at + 1]
                )
                joined[n, :, cols] = merged.astype(jnp.bfloat16)
            remote(
                joined.at[n, :, piece(chunk)],
                text_back.at[HALVES, :, part_cols(column, chunk)],
                "joined",
                final_recv.at[0],
                there + n,
            ).start()

    neighbours = (
        *((1, COLUMNS * near_place + side) for side in range(COLUMNS)),
        (0, beside),
    )

    def inbound_send(chunk, later):
        rows_of = inbound_half(chunk, later)
        remote(
            text_part.at[pl.ds(there + rows_of.start, rows_of.size), :, piece(chunk)],
            inbound.at[rows_of, :, piece(chunk)],
            "inbound",
            inbound_recv.at[0, chunk + later],
            near,
        ).start()

    def text_chunk(chunk, role):
        if role == "outer":
            for _n in far_waits(chunk):
                pass
        with jax.named_scope(f"q_near{chunk}"):
            take(text_rows.at[pl.ds(0, 2), :, piece(chunk)], query_recv.at[1, chunk])
        with jax.named_scope(f"kv{chunk}"):
            take(context.at[0, :, :, piece(chunk)], context_recv.at[chunk])
        tops, totals = jnp.full((query_total, HEAD_DIM), FAR, jnp.float32), 1.0

        def loads(head):
            cols = slice(head * HEAD_DIM, (head + 1) * HEAD_DIM)
            return (
                text_rows[:, :, cols].reshape(query_total, HEAD_DIM),
                context[:, 0, :, cols].reshape(key_total, HEAD_DIM),
                context[:, 1, :, cols].reshape(key_total, HEAD_DIM),
            )

        heads = range(chunk * chunk_heads, (chunk + 1) * chunk_heads)
        for head, mixed, top, total in attend(loads, heads, live):
            cols = slice(head * HEAD_DIM, (head + 1) * HEAD_DIM)
            share = mixed.reshape(count, rows, HEAD_DIM)
            text_full[:, :, cols] = share
            text_part[:, :, cols] = share.astype(jnp.bfloat16)
            tops = jnp.where(lane == head, top, tops)
            totals = jnp.where(lane == head, total, totals)
        if role == "outer":
            inbound_send(chunk, 0)
        levels = (tops * SCALE + jnp.log2(totals)).reshape(count, rows, HEAD_DIM)
        if chunk:
            before = lax.broadcasted_iota(jnp.int32, (1, 1, HEAD_DIM), 2) < chunk * chunk_heads
            levels = jnp.where(before, stat_part[...], levels)
        stat_part[...] = levels
        if role == "outer":
            stat_pack[chunk] = gathered()
            remote(
                stat_pack.at[chunk], stat_in.at[chunk], "inbound_stat", inbound_recv.at[1, chunk], near
            ).start()
            if chunk == CHUNKS - 1:
                inbound_send(chunk, 1)

    def near_send(low, high):
        for slot, device in neighbours:
            remote(
                text_part.at[device, :, piece(low, high + 1 - low)],
                text_back.at[slot, :, part_cols(column, low, high + 1 - low)],
                "near",
                final_recv.at[0],
                device,
            ).start()

    def near_stats():
        for slot, device in neighbours:
            remote(
                stat_part.at[device], stat_back.at[slot, column], "near_stat", final_recv.at[1], device
            ).start()

    def self_attention():
        take(own.at[pl.ds(0, 3)], local_sem.at[2])
        with jax.named_scope("self"):
            take(own.at[pl.ds(0, 3 * (count - 1))], final_recv.at[3])

        def loads(head):
            cols = slice(head * HEAD_DIM, (head + 1) * HEAD_DIM)
            return [
                own[kind * count : (kind + 1) * count, :, cols].reshape(query_total, HEAD_DIM)
                for kind in range(3)
            ]

        for head, mixed, _, _ in attend(loads, range(self_heads), None):
            cols = slice(head * HEAD_DIM, (head + 1) * HEAD_DIM)
            self_part[:, :, cols] = mixed.astype(jnp.bfloat16).reshape(count, rows, HEAD_DIM)
        for n in range(count - 1):
            to = n + lax.div(n + count - me, count)
            remote(
                self_part.at[to], self_out.at[0, :, self_cols(me)], "self_return", final_recv.at[2], to
            ).start()

    def relay():
        for chunk in range(CHUNKS):
            for n, origin in far_waits(chunk):
                query_copy("relay", 2 + n, chunk, held(origin, chunk), origin, near).start()

    def run(role, steps):
        for step in steps:
            name, _, only = step.partition(".")
            kind, digits = name[0], [int(digit) for digit in name[1:]]
            action = {
                "b": start_self,
                "x": context_send,
                "c": functools.partial(text_chunk, role=role),
                "n": near_send,
                "j": join,
                "r": relay,
                "t": near_stats,
                "s": self_attention,
            }[kind]
            if only:
                holds = half == int(only[1:]) if only[0] == "h" else branch == int(only)
                pl.when(holds)(functools.partial(action, *digits))
            else:
                action(*digits)

    kept_context.wait()

    @pl.when(outer)
    def _():
        run("outer", OUTER)

    @pl.when(inner)
    def _():
        stat_sum[...] = jnp.zeros_like(stat_sum)
        run("inner", INNER)

    kept_part = pltpu.make_async_copy(text_full.at[me], own_back, local_sem.at[0])
    kept_stat = pltpu.make_async_copy(stat_part.at[me], stat_back.at[0, column], local_sem.at[1])
    kept_self = pltpu.make_async_copy(self_part.at[me], self_out.at[0, :, self_cols(me)], local_sem.at[2])
    kept_part.start()
    kept_stat.start()
    kept_self.start()
    kept_part.wait()
    kept_stat.wait()
    kept_self.wait()
    with jax.named_scope("back"):
        take(text_part.at[pl.ds(0, 3 + COLUMNS)], final_recv.at[0])
    with jax.named_scope("back_stat"):
        take(stat_part.at[pl.ds(0, 3 + COLUMNS)], final_recv.at[1])
    with jax.named_scope("self_out"):
        take(self_part.at[pl.ds(0, count - 1)], final_recv.at[2])
    with jax.named_scope("sends"):
        take(text_full, sends.at[0])
        take(text_rows.at[pl.ds(0, count - 1)], sends.at[1])
        take(stat_part.at[pl.ds(0, count - 1)], sends.at[3])

    @pl.when(outer)
    def _():
        take(inbound, sends.at[2])

    @pl.when(inner)
    def _():
        take(text_rows, sends.at[2])


def settle(self_in, text_in, stat_in, own_in, self_out, text_out, mixed, out_sem):
    column = lax.rem(lax.axis_index("seq"), COLUMNS)
    text_span = own_in.shape[1]
    leaving = [pltpu.make_async_copy(self_in, self_out, out_sem.at[0])]
    leaving[0].start()
    for side in range(COLUMNS):
        sides = [stat_in[n, side] for n in range(HALVES + 1)]
        highest = functools.reduce(jnp.maximum, sides)
        shares = [jnp.exp2(each - highest) for each in sides]
        whole = sum(shares)
        shares = [share / whole for share in shares]
        for head in range(text_span // HEAD_DIM):
            cols = slice(side * text_span + head * HEAD_DIM, side * text_span + (head + 1) * HEAD_DIM)
            here = jnp.where(
                column == side,
                own_in[:, head * HEAD_DIM : (head + 1) * HEAD_DIM],
                text_in[0, :, cols].astype(jnp.float32),
            )
            merged = here * shares[0][:, head : head + 1] + sum(
                text_in[n, :, cols].astype(jnp.float32) * shares[n][:, head : head + 1]
                for n in range(1, HALVES + 1)
            )
            mixed[0, :, cols] = merged.astype(jnp.bfloat16)
        piece = pl.ds(side * text_span, text_span)
        leaving.append(
            pltpu.make_async_copy(mixed.at[:, :, piece], text_out.at[:, :, piece], out_sem.at[1 + side])
        )
        leaving[1 + side].start()
    for copy in leaving:
        copy.wait()


def fused_shards(self_queries, self_keys, self_values, text_queries, text_kv, text_len):
    count = lax.axis_size("seq")
    rows, channels = self_queries.shape[1:]
    context_rows = text_kv.shape[2]
    span = count // HALVES
    self_span, text_span = channels // count, channels // COLUMNS
    operands = (self_queries, self_keys, self_values, text_queries, text_kv, text_len)
    in_place = pl.BlockSpec(memory_space=pl.ANY)
    bf16, f32 = jnp.bfloat16, jnp.float32
    out = jax.ShapeDtypeStruct((1, rows, channels), bf16)
    dma = pltpu.SemaphoreType.DMA
    results = pl.pallas_call(
        functools.partial(fused, count),
        out_shape=(
            out,
            jax.ShapeDtypeStruct((HALVES + 1, rows, channels), bf16),
            jax.ShapeDtypeStruct((HALVES + 1, COLUMNS, rows, HEAD_DIM), f32),
            jax.ShapeDtypeStruct((rows, text_span), f32),
        ),
        in_specs=[in_place] * 6,
        out_specs=(in_place,) * 4,
        scratch_shapes=[
            pltpu.VMEM((3 * count, rows, self_span), bf16),
            pltpu.VMEM((count, rows, self_span), bf16),
            pltpu.VMEM((count, rows, text_span), bf16),
            pltpu.VMEM((COLUMNS, 2, context_rows, text_span), bf16),
            pltpu.VMEM((count, rows, text_span), bf16),
            pltpu.VMEM((count, rows, text_span), f32),
            pltpu.VMEM((span, rows, text_span), bf16),
            pltpu.VMEM((span, rows, text_span), bf16),
            pltpu.VMEM((count, rows, HEAD_DIM), f32),
            pltpu.VMEM((CHUNKS, rows, HEAD_DIM), f32),
            pltpu.VMEM((CHUNKS, rows, HEAD_DIM), f32),
            pltpu.VMEM((span, rows, HEAD_DIM), f32),
            pltpu.VMEM((rows, HEAD_DIM), f32),
            pltpu.SMEM(text_len.shape, jnp.int32),
            dma((2 + span, CHUNKS)),
            dma((CHUNKS,)),
            dma((2, CHUNKS + 1)),
            dma((4,)),
            dma((4,)),
            dma((4,)),
        ],
        compiler_params=pltpu.CompilerParams(
            collective_id=0, has_side_effects=True, vmem_limit_bytes=GRANT
        ),
        name="attention",
    )(*[pltpu.with_memory_space_constraint(each, pltpu.HBM) for each in operands])
    return pl.pallas_call(
        settle,
        out_shape=(out, out),
        in_specs=[pl.BlockSpec(memory_space=pltpu.VMEM)] * 4,
        out_specs=(in_place, in_place),
        scratch_shapes=[pltpu.VMEM((1, rows, channels), bf16), dma((1 + COLUMNS,))],
        compiler_params=pltpu.CompilerParams(vmem_limit_bytes=GRANT),
        name="settle",
    )(*results)


def solution(mesh):
    count = mesh.shape["seq"]
    fits = count == COLUMNS * PLACES and HEADS % count == 0
    return jax.shard_map(
        fused_shards if fits else shards,
        mesh=mesh,
        in_specs=(
            P("enc", ("groups", "seq"), None),
            P("enc", ("groups", "seq"), None),
            P("enc", ("groups", "seq"), None),
            P("enc", ("groups", "seq"), None),
            P("enc", None, ("groups", "seq"), None),
            P("groups"),
        ),
        out_specs=(P("enc", ("groups", "seq"), None), P("enc", ("groups", "seq"), None)),
        check_vma=False,
    )
```

```python
import functools
import math

import jax
import jax.numpy as jnp
from jax import lax
from jax.experimental import pallas as pl
from jax.experimental.pallas import tpu as pltpu
from jax.sharding import PartitionSpec as P

HEADS = 32
HEAD_DIM = 128


def absorb(run_state, queries, key_rows, value_rows, live_mask):
    running_max, row_total, weighted_sum = run_state
    scores = jnp.einsum(
        "qpd,kpd->pqk", queries, key_rows, preferred_element_type=jnp.float32
    ) / math.sqrt(HEAD_DIM)
    scores = jnp.where(live_mask[None, None, :], scores, -1e30)
    new_max = jnp.maximum(running_max, jnp.max(scores, axis=2))
    weights = jnp.where(live_mask[None, None, :], jnp.exp(scores - new_max[:, :, None]), 0.0)
    factor = jnp.exp(running_max - new_max)
    row_total = row_total * factor + jnp.sum(weights, axis=2)
    weighted_sum = weighted_sum * factor[:, :, None] + jnp.einsum(
        "pqk,kpd->pqd", weights.astype(jnp.bfloat16), value_rows, preferred_element_type=jnp.float32
    )
    return (new_max, row_total, weighted_sum)


def empty_state(head_count, query_count):
    return (
        jnp.full((head_count, query_count), -1e30, jnp.float32),
        jnp.zeros((head_count, query_count), jnp.float32),
        jnp.zeros((head_count, query_count, HEAD_DIM), jnp.float32),
    )


def finish(run_state):
    running_max, row_total, weighted_sum = run_state
    return (weighted_sum / row_total[:, :, None]).transpose(1, 0, 2).astype(jnp.bfloat16)


def block_attention(queries, key_rows, value_rows, live_mask):
    query_total, heads_here, head_width = queries.shape
    key_total = key_rows.shape[0]
    key_block = 1024 if key_total % 1024 == 0 else key_total
    query_block = 512 if query_total % 512 == 0 else query_total
    key_blocks = key_rows.reshape(key_total // key_block, key_block, heads_here, head_width)
    value_blocks = value_rows.reshape(key_total // key_block, key_block, heads_here, head_width)
    live_blocks = live_mask.reshape(key_total // key_block, key_block)

    def one_block(query_piece):

        def absorb_block(run_state, pieces):
            return (absorb(run_state, query_piece, pieces[0], pieces[1], pieces[2]), None)

        final_state, unused = lax.scan(
            absorb_block,
            empty_state(heads_here, query_block),
            (key_blocks, value_blocks, live_blocks),
        )
        return finish(final_state)

    blended = lax.map(
        one_block, queries.reshape(query_total // query_block, query_block, heads_here, head_width)
    )
    return blended.reshape(query_total, heads_here, head_width)


def shards(self_queries, self_keys, self_values, text_queries, text_kv, text_len):
    token_rows = self_queries.shape[1]
    channel_count = self_queries.shape[2]
    seq_count = lax.axis_size("seq")
    quarter_count = max(seq_count // HEADS, 1)
    heads_here = max(HEADS // seq_count, 1)
    group_count = HEADS // heads_here
    head_span = heads_here * HEAD_DIM
    share_rows = token_rows // quarter_count
    query_total = share_rows * seq_count
    branch = lax.axis_index("enc")
    length = lax.dynamic_index_in_dim(text_len, branch, 0, keepdims=False)

    def head_view(tensor):
        return tensor.reshape(1, share_rows, seq_count, head_span)

    def repeated(tensor):
        spread = jnp.broadcast_to(
            tensor.reshape(1, token_rows, 1, group_count, head_span),
            (1, token_rows, quarter_count, group_count, head_span),
        )
        return spread.reshape(1, token_rows, seq_count, head_span)

    head_queries, head_keys, head_values = (
        lax.all_to_all(head_view(self_queries), "seq", split_axis=2, concat_axis=1, tiled=True),
        lax.all_to_all(repeated(self_keys), "seq", split_axis=2, concat_axis=1, tiled=True),
        lax.all_to_all(repeated(self_values), "seq", split_axis=2, concat_axis=1, tiled=True),
    )
    key_rows = head_keys.reshape(-1, heads_here, HEAD_DIM)
    value_rows = head_values.reshape(-1, heads_here, HEAD_DIM)
    query_rows = head_queries.reshape(query_total, heads_here, HEAD_DIM)
    every_key = jnp.ones((key_rows.shape[0],), jnp.bool_)
    self_heads = block_attention(query_rows, key_rows, value_rows, every_key)
    head_text_queries = lax.all_to_all(
        head_view(text_queries), "seq", split_axis=2, concat_axis=1, tiled=True
    )
    context_rows = text_kv.shape[2]
    spread = jnp.broadcast_to(
        text_kv.reshape(1, 2, context_rows, 1, group_count, head_span),
        (1, 2, context_rows, quarter_count, group_count, head_span),
    )
    head_context = lax.all_to_all(
        spread.reshape(1, 2, context_rows, seq_count, head_span),
        "seq",
        split_axis=3,
        concat_axis=2,
        tiled=True,
    )
    text_total = head_context.shape[2]
    context_keys = head_context[0, 0].reshape(text_total, heads_here, HEAD_DIM)
    context_values = head_context[0, 1].reshape(text_total, heads_here, HEAD_DIM)
    live_mask = jnp.arange(text_total, dtype=jnp.int32) < length
    text_heads = block_attention(
        head_text_queries.reshape(query_total, heads_here, HEAD_DIM),
        context_keys,
        context_values,
        live_mask,
    )
    self_view = self_heads.reshape(1, seq_count, share_rows, 1, head_span)
    text_view = text_heads.reshape(1, seq_count, share_rows, 1, head_span)
    self_back, text_back = (
        lax.all_to_all(self_view, "seq", split_axis=1, concat_axis=3, tiled=True),
        lax.all_to_all(text_view, "seq", split_axis=1, concat_axis=3, tiled=True),
    )
    self_mixed = self_back.reshape(1, token_rows, channel_count)
    text_mixed = text_back.reshape(1, token_rows, channel_count)
    return (self_mixed, text_mixed)


COLUMNS = 2
HALVES = 2
PLACES = 4
CHUNKS = 4
WRITE_HEADS = 8
GRANT = 12 * 1024 * 1024
SENDS = {"query": 0, "context": 0, "near": 0, "self": 1, "self_return": 1}
SENDS |= {"relay": 2, "joined": 2, "inbound": 2, "near_stat": 3, "inbound_stat": 3, "joined_stat": 3}
OUTER = ('b2.0', 'b2.1', 'b4.0', 'b6.1', 'c0', 'b6.0', 'b4.1', 'b7.0', 'b7.1', 'b5.0', 'b5.1', 'b3.1', 'b1.0', 'b1.1', 'b3.0', 'c1', 'c2', 'c3', 't.h0', 'n01.h0', 'n23.h0', 's', 'n01.h1', 'n23.h1', 't.h1')
INNER = ('b6', 'r', 'b2', 'b4.1', 'c0', 'b4.0', 'b7', 'b5', 'b3', 'b1', 'c1', 'n01.h0', 'c2', 'n22.h0', 'j0', 'c3', 't.h0', 'n33.h0', 'j1', 's', 'j2', 'j3', 'n01.h1', 'n23.h1', 't.h1')
FIRST_OUTER, FIRST_INNER = (), ()
LATER = tuple(sorted(int(step[1]) for step in OUTER if step[0] == "x"))
MESH = pl.DeviceIdType.MESH
FAR = -1e30
SCALE = math.log2(math.e) / math.sqrt(HEAD_DIM)


def attend(loads, heads, live):
    scores, sides = {}, {}
    for head in heads:
        queries, key_rows, _ = loads(head)
        scores[head] = lax.dot_general(
            queries, key_rows, (((1,), (1,)), ((), ())), preferred_element_type=jnp.float32
        )
    for head in heads:
        held = scores[head] if live is None else jnp.where(live, scores[head], FAR)
        top = jnp.max(held, axis=1, keepdims=True)
        weights = jnp.exp2((held - top) * SCALE)
        sides[head] = weights.astype(jnp.bfloat16), top, jnp.sum(weights, axis=1, keepdims=True)
    for head in heads:
        weights, top, total = sides[head]
        mixed = jnp.dot(weights, loads(head)[2], preferred_element_type=jnp.float32)
        yield head, mixed / total, top, total


def fused(
    count,
    self_q,
    self_k,
    self_v,
    text_q,
    text_kv,
    text_len,
    self_out,
    text_back,
    stat_back,
    own_back,
    own,
    self_part,
    text_rows,
    context,
    text_part,
    text_full,
    inbound,
    joined,
    stat_part,
    stat_pack,
    stat_in,
    stat_join,
    stat_sum,
    live_len,
    query_recv,
    context_recv,
    inbound_recv,
    final_recv,
    sends,
    local_sem,
):
    me = lax.axis_index("seq")
    branch = lax.axis_index("enc")
    place, column = lax.div(me, COLUMNS), lax.rem(me, COLUMNS)
    half = lax.div(place, PLACES // HALVES)
    span = count // HALVES
    inner = lax.rem(place, 2) + half == 1
    outer = lax.rem(place, 2) + half != 1
    beside = COLUMNS * place + 1 - column
    near_place = place + 1 - 2 * lax.rem(place, 2)
    near, near_beside = COLUMNS * near_place + column, COLUMNS * near_place + 1 - column
    inner_there, outer_there = 2 - half, (PLACES - 1) * (1 - half)
    across = COLUMNS * inner_there + column
    there = (1 - half) * span
    rows = self_q.shape[1]
    query_total = count * rows
    context_rows = text_kv.shape[2]
    key_total = COLUMNS * context_rows
    self_span = own.shape[2]
    text_span = text_rows.shape[2]
    self_heads, text_heads = self_span // HEAD_DIM, text_span // HEAD_DIM
    chunk_heads = text_heads // CHUNKS
    chunk_span = chunk_heads * HEAD_DIM
    send_of = {name: sends.at[n] for name, n in SENDS.items()}

    def self_cols(device):
        return pl.ds(pl.multiple_of(device * self_span, self_span), self_span)

    def text_cols(side):
        return pl.ds(pl.multiple_of(side * text_span, text_span), text_span)

    def part_cols(side, chunk, width=1):
        return pl.ds(pl.multiple_of(side * text_span + chunk * chunk_span, chunk_span), width * chunk_span)

    def piece(chunk, width=1):
        return pl.ds(chunk * chunk_span, width * chunk_span)

    def remote(source, target, kind, recv, device):
        return pltpu.make_async_remote_copy(
            src_ref=source,
            dst_ref=target,
            send_sem=send_of[kind],
            recv_sem=recv,
            device_id={"seq": device},
            device_id_type=MESH,
        )

    def take(ref, sem):
        pltpu.make_async_copy(ref, ref, sem).wait()

    def start(copies):
        for copy in copies:
            copy.start()

    def mirror(bits):
        far_place = (
            place,
            near_place,
            lax.rem(place + 2, PLACES),
            PLACES - 1 - place,
        )[bits // 2]
        return COLUMNS * far_place + (column if bits % 2 == 0 else 1 - column)

    barrier = pltpu.get_barrier_semaphore()
    for step in range(1, count):
        pl.semaphore_signal(
            barrier, inc=1, device_id={"seq": lax.rem(me + step, count)}, device_id_type=MESH
        )
    with jax.named_scope("entry"):
        pl.semaphore_wait(barrier, count - 1)

    def held(origin, chunk):
        return text_rows.at[origin, :, piece(chunk)]

    def query_copy(kind, slot, chunk, source, origin, device):
        return remote(source, held(origin, chunk), kind, query_recv.at[slot, chunk], device)

    origins = [
        COLUMNS * inner_there + column,
        COLUMNS * outer_there + column,
        COLUMNS * inner_there + 1 - column,
        COLUMNS * outer_there + 1 - column,
    ]
    first = 2 + lax.rem(lax.rem(place, 2) + half + 1, 2)
    for chunk in range(CHUNKS):
        query_copy(
            "query", 0, chunk, text_q.at[0, :, part_cols(1 - column, chunk)], me, beside
        ).start()
    for chunk in range(CHUNKS):
        mine = text_q.at[0, :, part_cols(column, chunk)]
        query_copy("query", first, chunk, mine, me, across).start()
    for chunk in range(CHUNKS):
        mine = text_q.at[0, :, part_cols(column, chunk)]
        query_copy("query", 1, chunk, mine, me, near).start()
    def context_send(chunk):
        remote(
            text_kv.at[0, :, :, part_cols(1 - column, chunk)],
            context.at[column, :, :, piece(chunk)],
            "context",
            context_recv.at[chunk],
            beside,
        ).start()

    for chunk in range(CHUNKS):
        if chunk not in LATER:
            context_send(chunk)

    @pl.when(branch == 0)
    def _():
        for chunk in LATER:
            context_send(chunk)

    kept_len = pltpu.make_async_copy(text_len, live_len, local_sem.at[3])
    kept_rows = pltpu.make_async_copy(text_q.at[0, :, text_cols(column)], text_rows.at[me], local_sem.at[0])
    kept_context = pltpu.make_async_copy(
        text_kv.at[0, :, :, text_cols(column)], context.at[column], local_sem.at[1]
    )
    kept_len.start()
    kept_rows.start()
    kept_context.start()
    for kind, source in enumerate((self_q, self_k, self_v)):
        pltpu.make_async_copy(
            source.at[0, :, self_cols(me)], own.at[kind * count + me], local_sem.at[2]
        ).start()

    def start_self(bits):
        to = mirror(bits)
        for kind, source in enumerate((self_q, self_k, self_v)):
            remote(
                source.at[0, :, self_cols(to)], own.at[kind * count + me], "self", final_recv.at[3], to
            ).start()

    for mask, steps in ((outer, FIRST_OUTER), (inner, FIRST_INNER)):

        @pl.when(mask)
        def _(steps=steps):
            for step in steps:
                start_self(int(step[1:]))

    for chunk in range(CHUNKS):
        with jax.named_scope(f"q_beside{chunk}"):
            take(held(beside, chunk), query_recv.at[0, chunk])
        query_copy("query", first + 2, chunk, held(beside, chunk), beside, across).start()
        query_copy("query", 1, chunk, held(beside, chunk), beside, near).start()

    def far_waits(chunk):
        for n, origin in enumerate(origins):
            with jax.named_scope(f"q_far{chunk}{n}"):
                take(held(origin, chunk), query_recv.at[2 + n, chunk])
            yield n, origin

    kept_rows.wait()

    kept_len.wait()
    length = live_len[branch]
    live = place * key_total + lax.broadcasted_iota(jnp.int32, (1, key_total), 1) < length
    lane = lax.broadcasted_iota(jnp.int32, (query_total, HEAD_DIM), 1)
    short_lane = lax.broadcasted_iota(jnp.int32, (rows, HEAD_DIM), 1)

    def gathered():
        packed = jnp.zeros((rows, HEAD_DIM), jnp.float32)
        for n in range(span):
            moved = stat_part[there + n]
            if n:
                moved = pltpu.roll(moved, n * text_heads, 1)
            packed = jnp.where(lax.div(short_lane, text_heads) == n, moved, packed)
        return packed

    def inbound_half(chunk, later):
        return pl.ds(0, span) if chunk < CHUNKS - 1 else pl.ds(later * span // 2, span // 2)

    def join(chunk):
        with jax.named_scope(f"inb{chunk}"):
            take(stat_in.at[chunk], inbound_recv.at[1, chunk])
            take(inbound.at[inbound_half(chunk, 0), :, piece(chunk)], inbound_recv.at[0, chunk])
        sides = [gathered(), stat_in[chunk]]
        highest = jnp.maximum(*sides)
        shares = [jnp.exp2(side - highest) for side in sides]
        whole = shares[0] + shares[1]
        shares = [share / whole for share in shares]
        ours = lax.div(lax.rem(short_lane, text_heads), chunk_heads) == chunk
        final = jnp.where(ours, highest + jnp.log2(whole), stat_sum[...])
        stat_sum[...] = final
        for n in range(span):
            if chunk == CHUNKS - 1:
                stat_join[n] = pltpu.roll(final, HEAD_DIM - n * text_heads, 1) if n else final
                remote(
                    stat_join.at[n],
                    stat_back.at[HALVES, column],
                    "joined_stat",
                    final_recv.at[1],
                    there + n,
                ).start()
        for n in range(span):
            if chunk == CHUNKS - 1 and n == span // 2:
                take(inbound.at[inbound_half(chunk, 1), :, piece(chunk)], inbound_recv.at[0, chunk + 1])
            for head in range(chunk * chunk_heads, (chunk + 1) * chunk_heads):
                cols = slice(head * HEAD_DIM, (head + 1) * HEAD_DIM)
                at = n * text_heads + head
                merged = (
                    text_full[there + n, :, cols] * shares[0][:, at : at + 1]
                    + inbound[n, :, cols].astype(jnp.float32) * shares[1][:, at : at + 1]
                )
                joined[n, :, cols] = merged.astype(jnp.bfloat16)
            remote(
                joined.at[n, :, piece(chunk)],
                text_back.at[HALVES, :, part_cols(column, chunk)],
                "joined",
                final_recv.at[0],
                there + n,
            ).start()

    neighbours = (
        *((1, COLUMNS * near_place + side) for side in range(COLUMNS)),
        (0, beside),
    )

    def inbound_send(chunk, later):
        rows_of = inbound_half(chunk, later)
        remote(
            text_part.at[pl.ds(there + rows_of.start, rows_of.size), :, piece(chunk)],
            inbound.at[rows_of, :, piece(chunk)],
            "inbound",
            inbound_recv.at[0, chunk + later],
            near,
        ).start()

    def text_chunk(chunk, role):
        if role == "outer":
            for _n in far_waits(chunk):
                pass
        with jax.named_scope(f"q_near{chunk}"):
            take(text_rows.at[pl.ds(0, 2), :, piece(chunk)], query_recv.at[1, chunk])
        with jax.named_scope(f"kv{chunk}"):
            take(context.at[0, :, :, piece(chunk)], context_recv.at[chunk])
        tops, totals = jnp.full((query_total, HEAD_DIM), FAR, jnp.float32), 1.0

        def loads(head):
            cols = slice(head * HEAD_DIM, (head + 1) * HEAD_DIM)
            return (
                text_rows[:, :, cols].reshape(query_total, HEAD_DIM),
                context[:, 0, :, cols].reshape(key_total, HEAD_DIM),
                context[:, 1, :, cols].reshape(key_total, HEAD_DIM),
            )

        heads = range(chunk * chunk_heads, (chunk + 1) * chunk_heads)
        for head, mixed, top, total in attend(loads, heads, live):
            cols = slice(head * HEAD_DIM, (head + 1) * HEAD_DIM)
            share = mixed.reshape(count, rows, HEAD_DIM)
            text_full[:, :, cols] = share
            text_part[:, :, cols] = share.astype(jnp.bfloat16)
            tops = jnp.where(lane == head, top, tops)
            totals = jnp.where(lane == head, total, totals)
        if role == "outer":
            inbound_send(chunk, 0)
        levels = (tops * SCALE + jnp.log2(totals)).reshape(count, rows, HEAD_DIM)
        if chunk:
            before = lax.broadcasted_iota(jnp.int32, (1, 1, HEAD_DIM), 2) < chunk * chunk_heads
            levels = jnp.where(before, stat_part[...], levels)
        stat_part[...] = levels
        if role == "outer":
            stat_pack[chunk] = gathered()
            remote(
                stat_pack.at[chunk], stat_in.at[chunk], "inbound_stat", inbound_recv.at[1, chunk], near
            ).start()
            if chunk == CHUNKS - 1:
                inbound_send(chunk, 1)

    def near_send(low, high):
        for slot, device in neighbours:
            remote(
                text_part.at[device, :, piece(low, high + 1 - low)],
                text_back.at[slot, :, part_cols(column, low, high + 1 - low)],
                "near",
                final_recv.at[0],
                device,
            ).start()

    def near_stats():
        for slot, device in neighbours:
            remote(
                stat_part.at[device], stat_back.at[slot, column], "near_stat", final_recv.at[1], device
            ).start()

    def self_attention():
        take(own.at[pl.ds(0, 3)], local_sem.at[2])
        with jax.named_scope("self"):
            take(own.at[pl.ds(0, 3 * (count - 1))], final_recv.at[3])

        def loads(head):
            cols = slice(head * HEAD_DIM, (head + 1) * HEAD_DIM)
            return [
                own[kind * count : (kind + 1) * count, :, cols].reshape(query_total, HEAD_DIM)
                for kind in range(3)
            ]

        for head, mixed, _, _ in attend(loads, range(self_heads), None):
            cols = slice(head * HEAD_DIM, (head + 1) * HEAD_DIM)
            self_part[:, :, cols] = mixed.astype(jnp.bfloat16).reshape(count, rows, HEAD_DIM)
        for n in range(count - 1):
            to = n + lax.div(n + count - me, count)
            remote(
                self_part.at[to], self_out.at[0, :, self_cols(me)], "self_return", final_recv.at[2], to
            ).start()

    def relay():
        for chunk in range(CHUNKS):
            for n, origin in far_waits(chunk):
                query_copy("relay", 2 + n, chunk, held(origin, chunk), origin, near).start()

    def run(role, steps):
        for step in steps:
            name, _, only = step.partition(".")
            kind, digits = name[0], [int(digit) for digit in name[1:]]
            action = {
                "b": start_self,
                "x": context_send,
                "c": functools.partial(text_chunk, role=role),
                "n": near_send,
                "j": join,
                "r": relay,
                "t": near_stats,
                "s": self_attention,
            }[kind]
            if only:
                holds = half == int(only[1:]) if only[0] == "h" else branch == int(only)
                pl.when(holds)(functools.partial(action, *digits))
            else:
                action(*digits)

    kept_context.wait()

    @pl.when(outer)
    def _():
        run("outer", OUTER)

    @pl.when(inner)
    def _():
        stat_sum[...] = jnp.zeros_like(stat_sum)
        run("inner", INNER)

    kept_part = pltpu.make_async_copy(text_full.at[me], own_back, local_sem.at[0])
    kept_stat = pltpu.make_async_copy(stat_part.at[me], stat_back.at[0, column], local_sem.at[1])
    kept_self = pltpu.make_async_copy(self_part.at[me], self_out.at[0, :, self_cols(me)], local_sem.at[2])
    kept_part.start()
    kept_stat.start()
    kept_self.start()
    kept_part.wait()
    kept_stat.wait()
    kept_self.wait()
    with jax.named_scope("back"):
        take(text_part.at[pl.ds(0, 3 + COLUMNS)], final_recv.at[0])
    with jax.named_scope("back_stat"):
        take(stat_part.at[pl.ds(0, 3 + COLUMNS)], final_recv.at[1])
    with jax.named_scope("self_out"):
        take(self_part.at[pl.ds(0, count - 1)], final_recv.at[2])
    with jax.named_scope("sends"):
        take(text_full, sends.at[0])
        take(text_rows.at[pl.ds(0, count - 1)], sends.at[1])
        take(stat_part.at[pl.ds(0, count - 1)], sends.at[3])

    @pl.when(outer)
    def _():
        take(inbound, sends.at[2])

    @pl.when(inner)
    def _():
        take(text_rows, sends.at[2])


def settle(self_in, text_in, stat_in, own_in, self_out, text_out, mixed, out_sem):
    column = lax.rem(lax.axis_index("seq"), COLUMNS)
    text_span = own_in.shape[1]
    leaving = [pltpu.make_async_copy(self_in, self_out, out_sem.at[0])]
    leaving[0].start()
    for side in range(COLUMNS):
        sides = [stat_in[n, side] for n in range(HALVES + 1)]
        highest = functools.reduce(jnp.maximum, sides)
        shares = [jnp.exp2(each - highest) for each in sides]
        whole = sum(shares)
        shares = [share / whole for share in shares]
        for head in range(text_span // HEAD_DIM):
            cols = slice(side * text_span + head * HEAD_DIM, side * text_span + (head + 1) * HEAD_DIM)
            here = jnp.where(
                column == side,
                own_in[:, head * HEAD_DIM : (head + 1) * HEAD_DIM],
                text_in[0, :, cols].astype(jnp.float32),
            )
            merged = here * shares[0][:, head : head + 1] + sum(
                text_in[n, :, cols].astype(jnp.float32) * shares[n][:, head : head + 1]
                for n in range(1, HALVES + 1)
            )
            mixed[0, :, cols] = merged.astype(jnp.bfloat16)
            if (head + 1) % WRITE_HEADS == 0:
                piece = pl.ds(cols.stop - WRITE_HEADS * HEAD_DIM, WRITE_HEADS * HEAD_DIM)
                copy = pltpu.make_async_copy(
                    mixed.at[:, :, piece], text_out.at[:, :, piece], out_sem.at[len(leaving)]
                )
                copy.start()
                leaving.append(copy)
    for copy in leaving:
        copy.wait()


def fused_shards(self_queries, self_keys, self_values, text_queries, text_kv, text_len):
    count = lax.axis_size("seq")
    rows, channels = self_queries.shape[1:]
    context_rows = text_kv.shape[2]
    span = count // HALVES
    self_span, text_span = channels // count, channels // COLUMNS
    operands = (self_queries, self_keys, self_values, text_queries, text_kv, text_len)
    in_place = pl.BlockSpec(memory_space=pl.ANY)
    bf16, f32 = jnp.bfloat16, jnp.float32
    out = jax.ShapeDtypeStruct((1, rows, channels), bf16)
    dma = pltpu.SemaphoreType.DMA
    results = pl.pallas_call(
        functools.partial(fused, count),
        out_shape=(
            out,
            jax.ShapeDtypeStruct((HALVES + 1, rows, channels), bf16),
            jax.ShapeDtypeStruct((HALVES + 1, COLUMNS, rows, HEAD_DIM), f32),
            jax.ShapeDtypeStruct((rows, text_span), f32),
        ),
        in_specs=[in_place] * 6,
        out_specs=(in_place,) * 4,
        scratch_shapes=[
            pltpu.VMEM((3 * count, rows, self_span), bf16),
            pltpu.VMEM((count, rows, self_span), bf16),
            pltpu.VMEM((count, rows, text_span), bf16),
            pltpu.VMEM((COLUMNS, 2, context_rows, text_span), bf16),
            pltpu.VMEM((count, rows, text_span), bf16),
            pltpu.VMEM((count, rows, text_span), f32),
            pltpu.VMEM((span, rows, text_span), bf16),
            pltpu.VMEM((span, rows, text_span), bf16),
            pltpu.VMEM((count, rows, HEAD_DIM), f32),
            pltpu.VMEM((CHUNKS, rows, HEAD_DIM), f32),
            pltpu.VMEM((CHUNKS, rows, HEAD_DIM), f32),
            pltpu.VMEM((span, rows, HEAD_DIM), f32),
            pltpu.VMEM((rows, HEAD_DIM), f32),
            pltpu.SMEM(text_len.shape, jnp.int32),
            dma((2 + span, CHUNKS)),
            dma((CHUNKS,)),
            dma((2, CHUNKS + 1)),
            dma((4,)),
            dma((4,)),
            dma((4,)),
        ],
        compiler_params=pltpu.CompilerParams(
            collective_id=0, has_side_effects=True, vmem_limit_bytes=GRANT
        ),
        name="attention",
    )(*[pltpu.with_memory_space_constraint(each, pltpu.HBM) for each in operands])
    return pl.pallas_call(
        settle,
        out_shape=(out, out),
        in_specs=[pl.BlockSpec(memory_space=pltpu.VMEM)] * 4,
        out_specs=(in_place, in_place),
        scratch_shapes=[pltpu.VMEM((1, rows, channels), bf16), dma((1 + HEADS // WRITE_HEADS,))],
        compiler_params=pltpu.CompilerParams(vmem_limit_bytes=GRANT),
        name="settle",
    )(*results)


def solution(mesh):
    count = mesh.shape["seq"]
    fits = count == COLUMNS * PLACES and HEADS % count == 0
    return jax.shard_map(
        fused_shards if fits else shards,
        mesh=mesh,
        in_specs=(
            P("enc", ("groups", "seq"), None),
            P("enc", ("groups", "seq"), None),
            P("enc", ("groups", "seq"), None),
            P("enc", ("groups", "seq"), None),
            P("enc", None, ("groups", "seq"), None),
            P("groups"),
        ),
        out_specs=(P("enc", ("groups", "seq"), None), P("enc", ("groups", "seq"), None)),
        check_vma=False,
    )
```

```python
import functools
import math

import jax
import jax.numpy as jnp
from jax import lax
from jax.experimental import pallas as pl
from jax.experimental.pallas import tpu as pltpu
from jax.sharding import PartitionSpec as P

HEADS = 32
HEAD_DIM = 128


def absorb(run_state, queries, key_rows, value_rows, live_mask):
    running_max, row_total, weighted_sum = run_state
    scores = jnp.einsum(
        "qpd,kpd->pqk", queries, key_rows, preferred_element_type=jnp.float32
    ) / math.sqrt(HEAD_DIM)
    scores = jnp.where(live_mask[None, None, :], scores, -1e30)
    new_max = jnp.maximum(running_max, jnp.max(scores, axis=2))
    weights = jnp.where(live_mask[None, None, :], jnp.exp(scores - new_max[:, :, None]), 0.0)
    factor = jnp.exp(running_max - new_max)
    row_total = row_total * factor + jnp.sum(weights, axis=2)
    weighted_sum = weighted_sum * factor[:, :, None] + jnp.einsum(
        "pqk,kpd->pqd", weights.astype(jnp.bfloat16), value_rows, preferred_element_type=jnp.float32
    )
    return (new_max, row_total, weighted_sum)


def empty_state(head_count, query_count):
    return (
        jnp.full((head_count, query_count), -1e30, jnp.float32),
        jnp.zeros((head_count, query_count), jnp.float32),
        jnp.zeros((head_count, query_count, HEAD_DIM), jnp.float32),
    )


def finish(run_state):
    running_max, row_total, weighted_sum = run_state
    return (weighted_sum / row_total[:, :, None]).transpose(1, 0, 2).astype(jnp.bfloat16)


def block_attention(queries, key_rows, value_rows, live_mask):
    query_total, heads_here, head_width = queries.shape
    key_total = key_rows.shape[0]
    key_block = 1024 if key_total % 1024 == 0 else key_total
    query_block = 512 if query_total % 512 == 0 else query_total
    key_blocks = key_rows.reshape(key_total // key_block, key_block, heads_here, head_width)
    value_blocks = value_rows.reshape(key_total // key_block, key_block, heads_here, head_width)
    live_blocks = live_mask.reshape(key_total // key_block, key_block)

    def one_block(query_piece):

        def absorb_block(run_state, pieces):
            return (absorb(run_state, query_piece, pieces[0], pieces[1], pieces[2]), None)

        final_state, unused = lax.scan(
            absorb_block,
            empty_state(heads_here, query_block),
            (key_blocks, value_blocks, live_blocks),
        )
        return finish(final_state)

    blended = lax.map(
        one_block, queries.reshape(query_total // query_block, query_block, heads_here, head_width)
    )
    return blended.reshape(query_total, heads_here, head_width)


def shards(self_queries, self_keys, self_values, text_queries, text_kv, text_len):
    token_rows = self_queries.shape[1]
    channel_count = self_queries.shape[2]
    seq_count = lax.axis_size("seq")
    quarter_count = max(seq_count // HEADS, 1)
    heads_here = max(HEADS // seq_count, 1)
    group_count = HEADS // heads_here
    head_span = heads_here * HEAD_DIM
    share_rows = token_rows // quarter_count
    query_total = share_rows * seq_count
    branch = lax.axis_index("enc")
    length = lax.dynamic_index_in_dim(text_len, branch, 0, keepdims=False)

    def head_view(tensor):
        return tensor.reshape(1, share_rows, seq_count, head_span)

    def repeated(tensor):
        spread = jnp.broadcast_to(
            tensor.reshape(1, token_rows, 1, group_count, head_span),
            (1, token_rows, quarter_count, group_count, head_span),
        )
        return spread.reshape(1, token_rows, seq_count, head_span)

    head_queries, head_keys, head_values = (
        lax.all_to_all(head_view(self_queries), "seq", split_axis=2, concat_axis=1, tiled=True),
        lax.all_to_all(repeated(self_keys), "seq", split_axis=2, concat_axis=1, tiled=True),
        lax.all_to_all(repeated(self_values), "seq", split_axis=2, concat_axis=1, tiled=True),
    )
    key_rows = head_keys.reshape(-1, heads_here, HEAD_DIM)
    value_rows = head_values.reshape(-1, heads_here, HEAD_DIM)
    query_rows = head_queries.reshape(query_total, heads_here, HEAD_DIM)
    every_key = jnp.ones((key_rows.shape[0],), jnp.bool_)
    self_heads = block_attention(query_rows, key_rows, value_rows, every_key)
    head_text_queries = lax.all_to_all(
        head_view(text_queries), "seq", split_axis=2, concat_axis=1, tiled=True
    )
    context_rows = text_kv.shape[2]
    spread = jnp.broadcast_to(
        text_kv.reshape(1, 2, context_rows, 1, group_count, head_span),
        (1, 2, context_rows, quarter_count, group_count, head_span),
    )
    head_context = lax.all_to_all(
        spread.reshape(1, 2, context_rows, seq_count, head_span),
        "seq",
        split_axis=3,
        concat_axis=2,
        tiled=True,
    )
    text_total = head_context.shape[2]
    context_keys = head_context[0, 0].reshape(text_total, heads_here, HEAD_DIM)
    context_values = head_context[0, 1].reshape(text_total, heads_here, HEAD_DIM)
    live_mask = jnp.arange(text_total, dtype=jnp.int32) < length
    text_heads = block_attention(
        head_text_queries.reshape(query_total, heads_here, HEAD_DIM),
        context_keys,
        context_values,
        live_mask,
    )
    self_view = self_heads.reshape(1, seq_count, share_rows, 1, head_span)
    text_view = text_heads.reshape(1, seq_count, share_rows, 1, head_span)
    self_back, text_back = (
        lax.all_to_all(self_view, "seq", split_axis=1, concat_axis=3, tiled=True),
        lax.all_to_all(text_view, "seq", split_axis=1, concat_axis=3, tiled=True),
    )
    self_mixed = self_back.reshape(1, token_rows, channel_count)
    text_mixed = text_back.reshape(1, token_rows, channel_count)
    return (self_mixed, text_mixed)


COLUMNS = 2
HALVES = 2
PLACES = 4
CHUNKS = 4
WRITE_HEADS = 8
GRANT = 12 * 1024 * 1024
SENDS = {"query": 0, "context": 0, "near": 0, "self": 1, "self_return": 1}
SENDS |= {"relay": 2, "joined": 2, "inbound": 2, "near_stat": 3, "inbound_stat": 3, "joined_stat": 3}
OUTER = ('b2.0', 'b2.1', 'b4.0', 'b6.1', 'c0', 'b6.0', 'b4.1', 'b7.0', 'b7.1', 'b5.0', 'b5.1', 'b3.1', 'b1.0', 'b1.1', 'b3.0', 'c1', 'c2', 'c3', 't.h0', 'n01.h0', 'n23.h0', 's', 'n01.h1', 'n23.h1', 't.h1')
INNER = ('b6', 'r', 'b2', 'b4.1', 'c0', 'b4.0', 'b7', 'b5', 'b3', 'b1', 'c1', 'n01.h0', 'c2', 'n22.h0', 'j0', 'c3', 't.h0', 'n33.h0', 'j1', 'j2', 's', 'j3', 'n01.h1', 'n23.h1', 't.h1')
FIRST_OUTER, FIRST_INNER = (), ()
LATER = tuple(sorted(int(step[1]) for step in OUTER if step[0] == "x"))
MESH = pl.DeviceIdType.MESH
FAR = -1e30
SCALE = math.log2(math.e) / math.sqrt(HEAD_DIM)


def attend(loads, heads, live):
    scores, sides = {}, {}
    for head in heads:
        queries, key_rows, _ = loads(head)
        scores[head] = lax.dot_general(
            queries, key_rows, (((1,), (1,)), ((), ())), preferred_element_type=jnp.float32
        )
    for head in heads:
        held = scores[head] if live is None else jnp.where(live, scores[head], FAR)
        top = jnp.max(held, axis=1, keepdims=True)
        weights = jnp.exp2((held - top) * SCALE)
        sides[head] = weights.astype(jnp.bfloat16), top, jnp.sum(weights, axis=1, keepdims=True)
    for head in heads:
        weights, top, total = sides[head]
        mixed = jnp.dot(weights, loads(head)[2], preferred_element_type=jnp.float32)
        yield head, mixed / total, top, total


def fused(
    count,
    self_q,
    self_k,
    self_v,
    text_q,
    text_kv,
    text_len,
    self_out,
    text_back,
    stat_back,
    own_back,
    own,
    self_part,
    text_rows,
    context,
    text_part,
    text_full,
    inbound,
    joined,
    stat_part,
    stat_pack,
    stat_in,
    stat_join,
    stat_sum,
    live_len,
    query_recv,
    context_recv,
    inbound_recv,
    final_recv,
    sends,
    local_sem,
):
    me = lax.axis_index("seq")
    branch = lax.axis_index("enc")
    place, column = lax.div(me, COLUMNS), lax.rem(me, COLUMNS)
    half = lax.div(place, PLACES // HALVES)
    span = count // HALVES
    inner = lax.rem(place, 2) + half == 1
    outer = lax.rem(place, 2) + half != 1
    beside = COLUMNS * place + 1 - column
    near_place = place + 1 - 2 * lax.rem(place, 2)
    near, near_beside = COLUMNS * near_place + column, COLUMNS * near_place + 1 - column
    inner_there, outer_there = 2 - half, (PLACES - 1) * (1 - half)
    across = COLUMNS * inner_there + column
    there = (1 - half) * span
    rows = self_q.shape[1]
    query_total = count * rows
    context_rows = text_kv.shape[2]
    key_total = COLUMNS * context_rows
    self_span = own.shape[2]
    text_span = text_rows.shape[2]
    self_heads, text_heads = self_span // HEAD_DIM, text_span // HEAD_DIM
    chunk_heads = text_heads // CHUNKS
    chunk_span = chunk_heads * HEAD_DIM
    send_of = {name: sends.at[n] for name, n in SENDS.items()}

    def self_cols(device):
        return pl.ds(pl.multiple_of(device * self_span, self_span), self_span)

    def text_cols(side):
        return pl.ds(pl.multiple_of(side * text_span, text_span), text_span)

    def part_cols(side, chunk, width=1):
        return pl.ds(pl.multiple_of(side * text_span + chunk * chunk_span, chunk_span), width * chunk_span)

    def piece(chunk, width=1):
        return pl.ds(chunk * chunk_span, width * chunk_span)

    def remote(source, target, kind, recv, device):
        return pltpu.make_async_remote_copy(
            src_ref=source,
            dst_ref=target,
            send_sem=send_of[kind],
            recv_sem=recv,
            device_id={"seq": device},
            device_id_type=MESH,
        )

    def take(ref, sem):
        pltpu.make_async_copy(ref, ref, sem).wait()

    def start(copies):
        for copy in copies:
            copy.start()

    def mirror(bits):
        far_place = (
            place,
            near_place,
            lax.rem(place + 2, PLACES),
            PLACES - 1 - place,
        )[bits // 2]
        return COLUMNS * far_place + (column if bits % 2 == 0 else 1 - column)

    barrier = pltpu.get_barrier_semaphore()
    for step in range(1, count):
        pl.semaphore_signal(
            barrier, inc=1, device_id={"seq": lax.rem(me + step, count)}, device_id_type=MESH
        )
    with jax.named_scope("entry"):
        pl.semaphore_wait(barrier, count - 1)

    def held(origin, chunk):
        return text_rows.at[origin, :, piece(chunk)]

    def query_copy(kind, slot, chunk, source, origin, device):
        return remote(source, held(origin, chunk), kind, query_recv.at[slot, chunk], device)

    origins = [
        COLUMNS * inner_there + column,
        COLUMNS * outer_there + column,
        COLUMNS * inner_there + 1 - column,
        COLUMNS * outer_there + 1 - column,
    ]
    first = 2 + lax.rem(lax.rem(place, 2) + half + 1, 2)
    for chunk in range(CHUNKS):
        query_copy(
            "query", 0, chunk, text_q.at[0, :, part_cols(1 - column, chunk)], me, beside
        ).start()
    for chunk in range(CHUNKS):
        mine = text_q.at[0, :, part_cols(column, chunk)]
        query_copy("query", first, chunk, mine, me, across).start()
    for chunk in range(CHUNKS):
        mine = text_q.at[0, :, part_cols(column, chunk)]
        query_copy("query", 1, chunk, mine, me, near).start()
    def context_send(chunk):
        remote(
            text_kv.at[0, :, :, part_cols(1 - column, chunk)],
            context.at[column, :, :, piece(chunk)],
            "context",
            context_recv.at[chunk],
            beside,
        ).start()

    for chunk in range(CHUNKS):
        if chunk not in LATER:
            context_send(chunk)

    @pl.when(branch == 0)
    def _():
        for chunk in LATER:
            context_send(chunk)

    kept_len = pltpu.make_async_copy(text_len, live_len, local_sem.at[3])
    kept_rows = pltpu.make_async_copy(text_q.at[0, :, text_cols(column)], text_rows.at[me], local_sem.at[0])
    kept_context = pltpu.make_async_copy(
        text_kv.at[0, :, :, text_cols(column)], context.at[column], local_sem.at[1]
    )
    kept_len.start()
    kept_rows.start()
    kept_context.start()
    for kind, source in enumerate((self_q, self_k, self_v)):
        pltpu.make_async_copy(
            source.at[0, :, self_cols(me)], own.at[kind * count + me], local_sem.at[2]
        ).start()

    def start_self(bits):
        to = mirror(bits)
        for kind, source in enumerate((self_q, self_k, self_v)):
            remote(
                source.at[0, :, self_cols(to)], own.at[kind * count + me], "self", final_recv.at[3], to
            ).start()

    for mask, steps in ((outer, FIRST_OUTER), (inner, FIRST_INNER)):

        @pl.when(mask)
        def _(steps=steps):
            for step in steps:
                start_self(int(step[1:]))

    for chunk in range(CHUNKS):
        with jax.named_scope(f"q_beside{chunk}"):
            take(held(beside, chunk), query_recv.at[0, chunk])
        query_copy("query", first + 2, chunk, held(beside, chunk), beside, across).start()
        query_copy("query", 1, chunk, held(beside, chunk), beside, near).start()

    def far_waits(chunk):
        for n, origin in enumerate(origins):
            with jax.named_scope(f"q_far{chunk}{n}"):
                take(held(origin, chunk), query_recv.at[2 + n, chunk])
            yield n, origin

    kept_rows.wait()

    kept_len.wait()
    length = live_len[branch]
    live = place * key_total + lax.broadcasted_iota(jnp.int32, (1, key_total), 1) < length
    lane = lax.broadcasted_iota(jnp.int32, (query_total, HEAD_DIM), 1)
    short_lane = lax.broadcasted_iota(jnp.int32, (rows, HEAD_DIM), 1)

    def gathered():
        packed = jnp.zeros((rows, HEAD_DIM), jnp.float32)
        for n in range(span):
            moved = stat_part[there + n]
            if n:
                moved = pltpu.roll(moved, n * text_heads, 1)
            packed = jnp.where(lax.div(short_lane, text_heads) == n, moved, packed)
        return packed

    def inbound_half(chunk, later):
        return pl.ds(0, span) if chunk < CHUNKS - 1 else pl.ds(later * span // 2, span // 2)

    def join(chunk):
        with jax.named_scope(f"inb{chunk}"):
            take(stat_in.at[chunk], inbound_recv.at[1, chunk])
            take(inbound.at[inbound_half(chunk, 0), :, piece(chunk)], inbound_recv.at[0, chunk])
        sides = [gathered(), stat_in[chunk]]
        highest = jnp.maximum(*sides)
        shares = [jnp.exp2(side - highest) for side in sides]
        whole = shares[0] + shares[1]
        shares = [share / whole for share in shares]
        ours = lax.div(lax.rem(short_lane, text_heads), chunk_heads) == chunk
        final = jnp.where(ours, highest + jnp.log2(whole), stat_sum[...])
        stat_sum[...] = final
        for n in range(span):
            if chunk == CHUNKS - 1:
                stat_join[n] = pltpu.roll(final, HEAD_DIM - n * text_heads, 1) if n else final
                remote(
                    stat_join.at[n],
                    stat_back.at[HALVES, column],
                    "joined_stat",
                    final_recv.at[1],
                    there + n,
                ).start()
        for n in range(span):
            if chunk == CHUNKS - 1 and n == span // 2:
                take(inbound.at[inbound_half(chunk, 1), :, piece(chunk)], inbound_recv.at[0, chunk + 1])
            for head in range(chunk * chunk_heads, (chunk + 1) * chunk_heads):
                cols = slice(head * HEAD_DIM, (head + 1) * HEAD_DIM)
                at = n * text_heads + head
                merged = (
                    text_full[there + n, :, cols] * shares[0][:, at : at + 1]
                    + inbound[n, :, cols].astype(jnp.float32) * shares[1][:, at : at + 1]
                )
                joined[n, :, cols] = merged.astype(jnp.bfloat16)
            remote(
                joined.at[n, :, piece(chunk)],
                text_back.at[HALVES, :, part_cols(column, chunk)],
                "joined",
                final_recv.at[0],
                there + n,
            ).start()

    neighbours = (
        *((1, COLUMNS * near_place + side) for side in range(COLUMNS)),
        (0, beside),
    )

    def inbound_send(chunk, later):
        rows_of = inbound_half(chunk, later)
        remote(
            text_part.at[pl.ds(there + rows_of.start, rows_of.size), :, piece(chunk)],
            inbound.at[rows_of, :, piece(chunk)],
            "inbound",
            inbound_recv.at[0, chunk + later],
            near,
        ).start()

    def text_chunk(chunk, role):
        if role == "outer":
            for _n in far_waits(chunk):
                pass
        with jax.named_scope(f"q_near{chunk}"):
            take(text_rows.at[pl.ds(0, 2), :, piece(chunk)], query_recv.at[1, chunk])
        with jax.named_scope(f"kv{chunk}"):
            take(context.at[0, :, :, piece(chunk)], context_recv.at[chunk])
        tops, totals = jnp.full((query_total, HEAD_DIM), FAR, jnp.float32), 1.0

        def loads(head):
            cols = slice(head * HEAD_DIM, (head + 1) * HEAD_DIM)
            return (
                text_rows[:, :, cols].reshape(query_total, HEAD_DIM),
                context[:, 0, :, cols].reshape(key_total, HEAD_DIM),
                context[:, 1, :, cols].reshape(key_total, HEAD_DIM),
            )

        heads = range(chunk * chunk_heads, (chunk + 1) * chunk_heads)
        for head, mixed, top, total in attend(loads, heads, live):
            cols = slice(head * HEAD_DIM, (head + 1) * HEAD_DIM)
            share = mixed.reshape(count, rows, HEAD_DIM)
            text_full[:, :, cols] = share
            text_part[:, :, cols] = share.astype(jnp.bfloat16)
            tops = jnp.where(lane == head, top, tops)
            totals = jnp.where(lane == head, total, totals)
        if role == "outer":
            inbound_send(chunk, 0)
        levels = (tops * SCALE + jnp.log2(totals)).reshape(count, rows, HEAD_DIM)
        if chunk:
            before = lax.broadcasted_iota(jnp.int32, (1, 1, HEAD_DIM), 2) < chunk * chunk_heads
            levels = jnp.where(before, stat_part[...], levels)
        stat_part[...] = levels
        if role == "outer":
            stat_pack[chunk] = gathered()
            remote(
                stat_pack.at[chunk], stat_in.at[chunk], "inbound_stat", inbound_recv.at[1, chunk], near
            ).start()
            if chunk == CHUNKS - 1:
                inbound_send(chunk, 1)

    def near_send(low, high):
        for slot, device in neighbours:
            remote(
                text_part.at[device, :, piece(low, high + 1 - low)],
                text_back.at[slot, :, part_cols(column, low, high + 1 - low)],
                "near",
                final_recv.at[0],
                device,
            ).start()

    def near_stats():
        for slot, device in neighbours:
            remote(
                stat_part.at[device], stat_back.at[slot, column], "near_stat", final_recv.at[1], device
            ).start()

    def self_attention():
        take(own.at[pl.ds(0, 3)], local_sem.at[2])
        with jax.named_scope("self"):
            take(own.at[pl.ds(0, 3 * (count - 1))], final_recv.at[3])

        def loads(head):
            cols = slice(head * HEAD_DIM, (head + 1) * HEAD_DIM)
            return [
                own[kind * count : (kind + 1) * count, :, cols].reshape(query_total, HEAD_DIM)
                for kind in range(3)
            ]

        for head, mixed, _, _ in attend(loads, range(self_heads), None):
            cols = slice(head * HEAD_DIM, (head + 1) * HEAD_DIM)
            self_part[:, :, cols] = mixed.astype(jnp.bfloat16).reshape(count, rows, HEAD_DIM)
        for n in range(count - 1):
            to = n + lax.div(n + count - me, count)
            remote(
                self_part.at[to], self_out.at[0, :, self_cols(me)], "self_return", final_recv.at[2], to
            ).start()

    def relay():
        for chunk in range(CHUNKS):
            for n, origin in far_waits(chunk):
                query_copy("relay", 2 + n, chunk, held(origin, chunk), origin, near).start()

    def run(role, steps):
        for step in steps:
            name, _, only = step.partition(".")
            kind, digits = name[0], [int(digit) for digit in name[1:]]
            action = {
                "b": start_self,
                "x": context_send,
                "c": functools.partial(text_chunk, role=role),
                "n": near_send,
                "j": join,
                "r": relay,
                "t": near_stats,
                "s": self_attention,
            }[kind]
            if only:
                holds = half == int(only[1:]) if only[0] == "h" else branch == int(only)
                pl.when(holds)(functools.partial(action, *digits))
            else:
                action(*digits)

    kept_context.wait()

    @pl.when(outer)
    def _():
        run("outer", OUTER)

    @pl.when(inner)
    def _():
        stat_sum[...] = jnp.zeros_like(stat_sum)
        run("inner", INNER)

    kept_part = pltpu.make_async_copy(text_full.at[me], own_back, local_sem.at[0])
    kept_stat = pltpu.make_async_copy(stat_part.at[me], stat_back.at[0, column], local_sem.at[1])
    kept_self = pltpu.make_async_copy(self_part.at[me], self_out.at[0, :, self_cols(me)], local_sem.at[2])
    kept_part.start()
    kept_stat.start()
    kept_self.start()
    kept_part.wait()
    kept_stat.wait()
    kept_self.wait()
    with jax.named_scope("back"):
        take(text_part.at[pl.ds(0, 3 + COLUMNS)], final_recv.at[0])
    with jax.named_scope("back_stat"):
        take(stat_part.at[pl.ds(0, 3 + COLUMNS)], final_recv.at[1])
    with jax.named_scope("self_out"):
        take(self_part.at[pl.ds(0, count - 1)], final_recv.at[2])
    with jax.named_scope("sends"):
        take(text_full, sends.at[0])
        take(text_rows.at[pl.ds(0, count - 1)], sends.at[1])
        take(stat_part.at[pl.ds(0, count - 1)], sends.at[3])

    @pl.when(outer)
    def _():
        take(inbound, sends.at[2])

    @pl.when(inner)
    def _():
        take(text_rows, sends.at[2])


def settle(self_in, text_in, stat_in, own_in, self_out, text_out, mixed, out_sem):
    column = lax.rem(lax.axis_index("seq"), COLUMNS)
    text_span = own_in.shape[1]
    leaving = [pltpu.make_async_copy(self_in, self_out, out_sem.at[0])]
    leaving[0].start()
    for side in range(COLUMNS):
        sides = [stat_in[n, side] for n in range(HALVES + 1)]
        highest = functools.reduce(jnp.maximum, sides)
        shares = [jnp.exp2(each - highest) for each in sides]
        whole = sum(shares)
        shares = [share / whole for share in shares]
        for head in range(text_span // HEAD_DIM):
            cols = slice(side * text_span + head * HEAD_DIM, side * text_span + (head + 1) * HEAD_DIM)
            here = jnp.where(
                column == side,
                own_in[:, head * HEAD_DIM : (head + 1) * HEAD_DIM],
                text_in[0, :, cols].astype(jnp.float32),
            )
            merged = here * shares[0][:, head : head + 1] + sum(
                text_in[n, :, cols].astype(jnp.float32) * shares[n][:, head : head + 1]
                for n in range(1, HALVES + 1)
            )
            mixed[0, :, cols] = merged.astype(jnp.bfloat16)
            if (head + 1) % WRITE_HEADS == 0:
                piece = pl.ds(cols.stop - WRITE_HEADS * HEAD_DIM, WRITE_HEADS * HEAD_DIM)
                copy = pltpu.make_async_copy(
                    mixed.at[:, :, piece], text_out.at[:, :, piece], out_sem.at[len(leaving)]
                )
                copy.start()
                leaving.append(copy)
    for copy in leaving:
        copy.wait()


def fused_shards(self_queries, self_keys, self_values, text_queries, text_kv, text_len):
    count = lax.axis_size("seq")
    rows, channels = self_queries.shape[1:]
    context_rows = text_kv.shape[2]
    span = count // HALVES
    self_span, text_span = channels // count, channels // COLUMNS
    operands = (self_queries, self_keys, self_values, text_queries, text_kv, text_len)
    in_place = pl.BlockSpec(memory_space=pl.ANY)
    bf16, f32 = jnp.bfloat16, jnp.float32
    out = jax.ShapeDtypeStruct((1, rows, channels), bf16)
    dma = pltpu.SemaphoreType.DMA
    results = pl.pallas_call(
        functools.partial(fused, count),
        out_shape=(
            out,
            jax.ShapeDtypeStruct((HALVES + 1, rows, channels), bf16),
            jax.ShapeDtypeStruct((HALVES + 1, COLUMNS, rows, HEAD_DIM), f32),
            jax.ShapeDtypeStruct((rows, text_span), f32),
        ),
        in_specs=[in_place] * 6,
        out_specs=(in_place,) * 4,
        scratch_shapes=[
            pltpu.VMEM((3 * count, rows, self_span), bf16),
            pltpu.VMEM((count, rows, self_span), bf16),
            pltpu.VMEM((count, rows, text_span), bf16),
            pltpu.VMEM((COLUMNS, 2, context_rows, text_span), bf16),
            pltpu.VMEM((count, rows, text_span), bf16),
            pltpu.VMEM((count, rows, text_span), f32),
            pltpu.VMEM((span, rows, text_span), bf16),
            pltpu.VMEM((span, rows, text_span), bf16),
            pltpu.VMEM((count, rows, HEAD_DIM), f32),
            pltpu.VMEM((CHUNKS, rows, HEAD_DIM), f32),
            pltpu.VMEM((CHUNKS, rows, HEAD_DIM), f32),
            pltpu.VMEM((span, rows, HEAD_DIM), f32),
            pltpu.VMEM((rows, HEAD_DIM), f32),
            pltpu.SMEM(text_len.shape, jnp.int32),
            dma((2 + span, CHUNKS)),
            dma((CHUNKS,)),
            dma((2, CHUNKS + 1)),
            dma((4,)),
            dma((4,)),
            dma((4,)),
        ],
        compiler_params=pltpu.CompilerParams(
            collective_id=0, has_side_effects=True, vmem_limit_bytes=GRANT
        ),
        name="attention",
    )(*[pltpu.with_memory_space_constraint(each, pltpu.HBM) for each in operands])
    return pl.pallas_call(
        settle,
        out_shape=(out, out),
        in_specs=[pl.BlockSpec(memory_space=pltpu.VMEM)] * 4,
        out_specs=(in_place, in_place),
        scratch_shapes=[pltpu.VMEM((1, rows, channels), bf16), dma((1 + HEADS // WRITE_HEADS,))],
        compiler_params=pltpu.CompilerParams(vmem_limit_bytes=GRANT),
        name="settle",
    )(*results)


def solution(mesh):
    count = mesh.shape["seq"]
    fits = count == COLUMNS * PLACES and HEADS % count == 0
    return jax.shard_map(
        fused_shards if fits else shards,
        mesh=mesh,
        in_specs=(
            P("enc", ("groups", "seq"), None),
            P("enc", ("groups", "seq"), None),
            P("enc", ("groups", "seq"), None),
            P("enc", ("groups", "seq"), None),
            P("enc", None, ("groups", "seq"), None),
            P("groups"),
        ),
        out_specs=(P("enc", ("groups", "seq"), None), P("enc", ("groups", "seq"), None)),
        check_vma=False,
    )
```
